32 devices in a mesh: dp: 16 (over z, y, core), head: 2 (over x).
Axes of the slice: x: 2, y: 2, z: 4, core: 2. Of those that a mesh axis runs over, the one named last changes fastest.
Arguments:
- tokens: bfloat16 [2, 16384, 768], P(None, ('dp', 'head')), may hold values from -6 to 6
- segment_ids: int32 [2, 32, 512], P(None, 'dp'), may hold values from 0 to 15, never falling along the last dimension, each value on 1 to 256 neighbouring positions
- w_qkv: bfloat16 [3, 768, 768], P(None, 'dp', 'head'), may hold values from -0.21875 to 0.21875
- qv_bias: float32 [2, 768], replicated, may hold values from -3 to 3
- w_out: bfloat16 [768, 768], P(None, ('dp', 'head')), may hold values from -0.875 to 0.875
- out_bias: float32 [768], replicated, may hold values from -3 to 3
- w_in: bfloat16 [768, 3072], P(None, ('dp', 'head')), may hold values from -0.21875 to 0.21875
- in_bias: float32 [3072], replicated, may hold values from -3 to 3
- w_back: bfloat16 [3072, 768], P(None, ('dp', 'head')), may hold values from -0.109375 to 0.109375
- back_bias: float32 [768], replicated, may hold values from -3 to 3
- norm_gains: float32 [2, 768], replicated, may hold values from 0.25 to 1.75
- norm_shifts: float32 [2, 768], replicated, may hold values from -2 to 2
- out_cotangent: bfloat16 [2, 16384, 768], P(None, ('dp', 'head')), may hold values from -6 to 6
Outputs:
- out: bfloat16 [2, 16384, 768], P(None, ('dp', 'head'))
- x_grad: float32 [2, 16384, 768], P(None, ('dp', 'head'))
- w_qkv_grad: float32 [3, 768, 768], P(None, 'dp', 'head')
- qv_bias_grad: float32 [2, 768], replicated
- w_out_grad: float32 [768, 768], P(None, ('dp', 'head'))
- out_bias_grad: float32 [768], replicated
- w_in_grad: float32 [768, 3072], P(None, ('dp', 'head'))
- in_bias_grad: float32 [3072], replicated
- w_back_grad: float32 [3072, 768], P(None, ('dp', 'head'))
- back_bias_grad: float32 [768], replicated
- norm_gains_grad: float32 [2, 768], replicated
- norm_shifts_grad: float32 [2, 768], replicated
The draws below stay inside these ranges and needn't reach their ends.
Inputs may be any that keep to these rules, and one draw needn't show every extreme that they name: `segment_ids`: within each packed row of 512 positions the ids never fall; a run of one id is at most 256 positions and one run in each row has that length.
All inputs are finite; a program needn't handle non-finite values.
Results may differ from the reference program's by a relative error of at most 0.014.
The reference program's roundings to bfloat16 on the way count: a program that leaves them out, or rounds other values in their place, can miss the bound.
Values may be sent and summed in bfloat16 or wider, within the bound.
A program may use at most 192 MiB of HBM per device.

```python
import math
import jax
import jax.numpy as jnp
import numpy as np
from jax import lax

D = 768
FF = 3072
H = 12
HD = 64
LEN = 512
MICRO = 2
SEQ_DP = 2
SEQS = 32
ROWS = 16384
N_DP = 16


def raised(values, key, source, target, blocks, factor):
    owner, partner = [(jnp.arange(values.shape[axis_at]) // (values.shape[axis_at] // blocks)).reshape([-1 if axis == axis_at else 1 for axis in range(values.ndim)]) for axis_at in (source, target)]
    chosen = jax.random.permutation(key, blocks)[partner]
    strong = (owner == chosen) | (owner == (partner + blocks // 2) % blocks)
    return jnp.where(strong, factor * values, values)


def block_levels(key, extent, shards, least, high):
    def one(position, parts):
        steps = jax.random.uniform(jax.random.fold_in(jax.random.fold_in(key, 6), position), (parts,), jnp.float32, least / len(shards), high / len(shards))
        return jnp.repeat(jnp.exp(steps), extent[position] // parts).reshape((-1,) + (1,) * (len(extent) - position - 1))

    loudness = one(*shards[0])
    for cut in shards[1:]:
        loudness = loudness * one(*cut)
    return loudness


def profile(number_of, total, most, skew):
    portions = [(1 << 20) // math.isqrt(standing ** skew) + 1 for standing in range(2, number_of + 1)]
    surplus, given = total - most - (number_of - 1), [1] * (number_of - 1)
    while surplus > 0:
        free = [i for i in range(number_of - 1) if given[i] < most]
        mass, left = sum([portions[i] for i in free]), surplus
        for i in free:
            more = min(most - given[i], max(1, left * portions[i] // mass), surplus)
            given[i] = given[i] + more
            surplus = surplus - more
    return np.array([most] + given)


def ragged_sizes(own_key, number_of, total, most, skew):
    if number_of == 2:
        one = jax.random.randint(own_key, (), max(1, total - most), min(most, total - 1) + 1)
        return jnp.stack([one, total - one])
    sizes = jnp.asarray(profile(number_of, total, most, skew), jnp.int32)
    pairs = (number_of - 1) // 2
    source_of, taker = sizes[1:1 + 2 * pairs:2], sizes[2:2 + 2 * pairs:2]
    slack = jnp.minimum(source_of - 1, most - taker)
    moved = jax.random.randint(jax.random.fold_in(own_key, 1), (pairs,), 0, 1 << 20) % (slack + 1)
    sizes = sizes.at[1:1 + 2 * pairs:2].set(source_of - moved).at[2:2 + 2 * pairs:2].set(taker + moved)
    return sizes[jax.random.permutation(jax.random.fold_in(own_key, 2), number_of)]


def bell_draw(key, dims, width, most, cuts=(), kind=jnp.bfloat16):
    drawn = jax.random.normal(key, dims, jnp.float32) * width
    if len(cuts) > 0:
        drawn = block_levels(key, dims, cuts, -0.22, 0.18) * drawn
    return jnp.clip(drawn, min=-most, max=most).astype(kind)


def bell_draw_with(key, extent, scale, limit, split, heavy, kind=jnp.bfloat16):
    values = scale * jax.random.normal(key, extent, jnp.float32)
    if split:
        values = values * block_levels(key, extent, split, -0.22, 0.18)
    return jnp.clip(raised(values, jax.random.fold_in(key, 3), *heavy), -limit, limit).astype(kind)


def setup_inputs(seed: int = 0) -> dict:
    key_list = jax.random.split(jax.random.key(seed), 14)
    tokens = bell_draw_with(key_list[0], (MICRO, ROWS, D), 1.0, 6.0, ((1, 32),), (1, 2, 32, 2.75))
    segment_ids = jax.vmap(lambda own: jnp.searchsorted(jnp.cumsum(ragged_sizes(own, max(4, LEN // 32), LEN, LEN // 2, 2)), jnp.arange(LEN), side="right"))(jax.random.split(key_list[1], MICRO * SEQS)).reshape((MICRO, SEQS, LEN)).astype(jnp.int32)
    w_qkv = bell_draw(key_list[2], (3, D, H * HD), D ** -0.5, 0.21875, ((1, 16), (2, 2)))
    qv_bias = bell_draw(key_list[3], (2, H * HD), 0.5, 3.0, (), jnp.float32)
    w_out = bell_draw(key_list[4], (H * HD, D), (H * HD // 16) ** -0.5, 0.875, ((1, 32),))
    out_bias = bell_draw(key_list[5], (D,), 0.5, 3.0, (), jnp.float32)
    w_in = bell_draw(key_list[6], (D, FF), D ** -0.5, 0.21875, ((1, 32),))
    in_bias = bell_draw(key_list[7], (FF,), 0.5, 3.0, (), jnp.float32)
    w_back = bell_draw(key_list[8], (FF, D), FF ** -0.5, 0.109375, ((1, 32),))
    back_bias = bell_draw(key_list[9], (D,), 0.5, 3.0, (), jnp.float32)
    norm_gains = jnp.clip(1.0 + 0.15 * jax.random.normal(key_list[10], (2, D), jnp.float32), 0.25, 1.75)
    norm_shifts = bell_draw(key_list[11], (2, D), 0.3, 2.0, (), jnp.float32)
    out_cotangent = bell_draw(key_list[12], (MICRO, ROWS, D), 1.0, 6.0, ((1, 32),))
    return dict(tokens=tokens, segment_ids=segment_ids, w_qkv=w_qkv, qv_bias=qv_bias, w_out=w_out, out_bias=out_bias, w_in=w_in, in_bias=in_bias, w_back=w_back, back_bias=back_bias, norm_gains=norm_gains, norm_shifts=norm_shifts, out_cotangent=out_cotangent)


@jax.custom_vjp
def low(v):
    return lax.optimization_barrier(v.astype(jnp.bfloat16)).astype(jnp.float32)

@jax.custom_vjp
def low_back(v):
    return v

def low_keep(v):
    return (low(v), None)

def low_pass(kept, grad):
    return (grad,)

def back_keep(v):
    return (v, None)

def back_low(kept, grad):
    return (low(grad),)
low.defvjp(low_keep, low_pass)
low_back.defvjp(back_keep, back_low)
PRECISE = lax.Precision.HIGHEST
NORM_EPS = 1e-05
MASKED = -1e+30

def matmul(left, right):
    return jnp.dot(left, right, precision=PRECISE)

def layer_norm(residual, norm_gain, offset):
    average = lax.optimization_barrier(jnp.mean(residual, axis=-1, keepdims=True))
    centred = residual - average
    spread = lax.optimization_barrier(jnp.mean(centred * centred, axis=-1, keepdims=True))
    return centred * lax.rsqrt(spread + NORM_EPS) * norm_gain + offset

def attend(block_items):
    queries, key_rows, values, segment = block_items
    raw_scores = jnp.einsum('qhd,khd->hqk', queries, key_rows, precision=PRECISE)
    scaled = low_back(raw_scores * HD ** (-0.5))
    same_doc = segment[:, None] == segment[None, :]
    scores = jnp.where(same_doc[None], scaled, MASKED)
    probabilities = jax.nn.softmax(scores, axis=-1)
    return jnp.einsum('hqk,khd->qhd', low(probabilities), values, precision=PRECISE)

def forward(param_set, inputs, segments):
    w_qkv, qv_bias, w_out, out_bias, w_in, in_bias, w_back, back_bias, norm_gain, norm_shift = param_set
    group_size = segments.shape[0]
    queries = low(low_back(matmul(inputs, w_qkv[0]) + qv_bias[0]))
    key_rows = low(low_back(matmul(inputs, w_qkv[1])))
    values = low(low_back(matmul(inputs, w_qkv[2]) + qv_bias[1]))
    head_shape = (group_size, LEN, H, HD)
    context = lax.map(jax.checkpoint(attend), (queries.reshape(head_shape), key_rows.reshape(head_shape), values.reshape(head_shape), segments))
    context = low(low_back(context.reshape(group_size * LEN, H * HD)))
    attended = low_back(matmul(context, w_out) + out_bias)
    hidden = layer_norm(inputs + attended, norm_gain[0], norm_shift[0])
    pre_act = low_back(matmul(low(hidden), w_in) + in_bias)
    activation = low(jax.nn.gelu(pre_act, approximate=False))
    branch = low_back(matmul(activation, w_back) + back_bias)
    return layer_norm(hidden + branch, norm_gain[1], norm_shift[1])

def reference(tokens, segment_ids, w_qkv, qv_bias, w_out, out_bias, w_in, in_bias, w_back, back_bias, norm_gains, norm_shifts, out_cotangent):
    group_size = math.gcd(SEQ_DP * N_DP, max(1, 4096 // LEN))
    blocks = MICRO * SEQ_DP * N_DP // group_size
    inputs = tokens.astype(jnp.float32).reshape(blocks, group_size * LEN, D)
    cotangents = out_cotangent.astype(jnp.float32).reshape(blocks, group_size * LEN, D)
    segments = segment_ids.reshape(blocks, group_size, LEN)
    params = tuple((array.astype(jnp.float32) for array in (w_qkv, qv_bias, w_out, out_bias, w_in, in_bias, w_back, back_bias, norm_gains, norm_shifts)))
    zero_grads = jax.tree.map(jnp.zeros_like, params)

    def step(totals, block_items):
        block_inputs, block_segments, block_cotangent = block_items

        def apply_block(param_set, layer_inputs):
            return forward(param_set, layer_inputs, block_segments)
        result, pullback = jax.vjp(apply_block, params, block_inputs)
        grad_params, grad_inputs = pullback(block_cotangent)
        return (jax.tree.map(jnp.add, totals, grad_params), (result.astype(jnp.bfloat16), grad_inputs))
    totals, (results, grad_inputs) = lax.scan(step, zero_grads, (inputs, segments, cotangents))
    return (results.reshape(MICRO, ROWS, D), grad_inputs.reshape(MICRO, ROWS, D), totals[0], totals[1], totals[2], totals[3], totals[4], totals[5], totals[6], totals[7], totals[8], totals[9])
```

```python
import functools
import math

import jax
import jax.numpy as jnp
from jax import lax
from jax.experimental import pallas as pl
from jax.experimental.pallas import tpu as pltpu
from jax.sharding import PartitionSpec as P

HD = 64
NORM_EPS = 1e-05
MASKED = -1e30
AXES = ("dp", "head")
F32 = jnp.float32
BF16 = jnp.bfloat16


def dot(left, right, left_dim, right_dim):
    return lax.dot_general(
        left, right, (((left_dim,), (right_dim,)), ((), ())), preferred_element_type=F32
    )


def fill_mask(segment_row, segment_col, mask_ref):
    @pl.when(pl.program_id(1) == 0)
    def _():
        mask_ref[...] = jnp.where(segment_col[0] == segment_row[0], 0.0, MASKED)


def lane_halves(rows):
    lane = lax.broadcasted_iota(jnp.int32, (rows, 2 * HD), 1)
    return lane < HD


def attend_kernel(seg_row, seg_col, qkv_ref, context_ref, total_ref, mask_ref):
    fill_mask(seg_row, seg_col, mask_ref)
    queries = qkv_ref[0] * jnp.asarray(HD**-0.5, BF16)
    key_rows = qkv_ref[1]
    values = qkv_ref[2]
    first = lane_halves(key_rows.shape[0])
    parts = []
    for head in range(2):
        keys_own = jnp.where(first if head == 0 else ~first, key_rows, jnp.zeros_like(key_rows))
        scores = dot(keys_own, queries, 1, 1) + mask_ref[...]
        highest = jnp.max(scores, axis=0, keepdims=True)
        exponent = jnp.exp(scores - highest)
        totals = jnp.sum(exponent, axis=0, keepdims=True)
        low = (exponent * (1.0 / totals)).astype(BF16)
        total_ref[0, 0, head : head + 1, :] = highest + jnp.log(totals)
        parts.append(dot(values, low, 0, 0))
    joined = jnp.concatenate([parts[0][:HD], parts[1][HD:]], axis=0)
    context_ref[...] = joined.T.astype(BF16)


def attend_back_kernel(seg_row, seg_col, qkv_ref, total_ref, grad_ref, out_ref, mask_ref):
    fill_mask(seg_row, seg_col, mask_ref)
    scale = jnp.asarray(HD**-0.5, BF16)
    queries = qkv_ref[0] * scale
    key_rows = qkv_ref[1]
    key_scaled = key_rows * scale
    values = qkv_ref[2]
    grad = grad_ref[...]
    first = lane_halves(key_rows.shape[0])
    grad_queries, grad_keys, grad_values = [], [], []
    for head in range(2):
        own = first if head == 0 else ~first
        zero = jnp.zeros_like(key_rows)
        scores = dot(jnp.where(own, key_rows, zero), queries, 1, 1) + mask_ref[...]
        probs = jnp.exp(scores - total_ref[0, 0, head : head + 1, :])
        grad_probs = dot(jnp.where(own, values, zero), grad, 1, 1)
        weighted = jnp.sum(probs * grad_probs, axis=0, keepdims=True)
        grad_scores = (probs * (grad_probs - weighted)).astype(BF16)
        grad_values.append(dot(probs.astype(BF16), grad, 1, 0))
        grad_keys.append(dot(grad_scores, queries, 1, 0))
        grad_queries.append(dot(key_scaled, grad_scores, 0, 0))
    joined = jnp.concatenate([grad_queries[0][:HD], grad_queries[1][HD:]], axis=0)
    out_ref[0] = joined.T.astype(BF16)
    out_ref[1] = jnp.where(first, grad_keys[0], grad_keys[1]).astype(BF16)
    out_ref[2] = jnp.where(first, grad_values[0], grad_values[1]).astype(BF16)


def attention_specs(seq_len):
    return dict(
        row=pl.BlockSpec((1, 1, seq_len), lambda r, h: (r, 0, 0)),
        col=pl.BlockSpec((1, seq_len, 1), lambda r, h: (r, 0, 0)),
        three=pl.BlockSpec((3, seq_len, 2 * HD), lambda r, h: (0, r, h)),
        one=pl.BlockSpec((seq_len, 2 * HD), lambda r, h: (r, h)),
        total=pl.BlockSpec((1, 1, 8, seq_len), lambda r, h: (r, h, 0, 0)),
    )


def attend(segments, qkv):
    rows, seq_len = segments.shape
    pairs = qkv.shape[2] // (2 * HD)
    s = attention_specs(seq_len)
    area = rows * pairs * 2 * seq_len * seq_len
    return pl.pallas_call(
        attend_kernel,
        grid=(rows, pairs),
        in_specs=[s["row"], s["col"], s["three"]],
        out_specs=[s["one"], s["total"]],
        out_shape=[
            jax.ShapeDtypeStruct(qkv.shape[1:], BF16),
            jax.ShapeDtypeStruct((rows, pairs, 8, seq_len), F32),
        ],
        scratch_shapes=[pltpu.VMEM((seq_len, seq_len), F32)],
        cost_estimate=pl.CostEstimate(
            flops=area * 512, bytes_accessed=qkv.size * 3, transcendentals=area
        ),
        name="attend",
    )(segments[:, None, :], segments[:, :, None], qkv)


def attend_back(segments, qkv, totals, grad):
    rows, seq_len = segments.shape
    pairs = qkv.shape[2] // (2 * HD)
    s = attention_specs(seq_len)
    area = rows * pairs * 2 * seq_len * seq_len
    return pl.pallas_call(
        attend_back_kernel,
        grid=(rows, pairs),
        in_specs=[s["row"], s["col"], s["three"], s["total"], s["one"]],
        out_specs=s["three"],
        out_shape=jax.ShapeDtypeStruct(qkv.shape, BF16),
        scratch_shapes=[pltpu.VMEM((seq_len, seq_len), F32)],
        cost_estimate=pl.CostEstimate(
            flops=area * 1280, bytes_accessed=qkv.size * 5, transcendentals=area
        ),
        name="attend_back",
    )(segments[:, None, :], segments[:, :, None], qkv, totals, grad)


def gelu_parts(value):
    size = jnp.abs(value)
    bell = jnp.exp(-0.5 * value * value)
    t = 1.0 / (1.0 + (0.3275911 / math.sqrt(2.0)) * size)
    series = 1.061405429 / 2
    for factor in (-1.453152027 / 2, 1.421413741 / 2, -0.284496736 / 2, 0.254829592 / 2):
        series = series * t + factor
    tail = series * t * bell
    cumulative = jnp.where(value < 0, tail, 1.0 - tail)
    return cumulative, value * bell * (1.0 / math.sqrt(2.0 * math.pi))


def norm_stats(residual):
    average = jnp.mean(residual, axis=-1, keepdims=True)
    centred = residual - average
    spread = jnp.mean(centred * centred, axis=-1, keepdims=True)
    inverse = lax.rsqrt(spread + NORM_EPS)
    return centred * inverse, inverse


def norm_back(normal, inverse, grad, gain):
    weighted = grad * gain
    along = jnp.mean(weighted * normal, axis=-1, keepdims=True)
    return inverse * (weighted - jnp.mean(weighted, axis=-1, keepdims=True) - normal * along)


def gather(shard):
    return lax.all_gather(shard, AXES, axis=0, tiled=True)


def reduce_rows(term):
    return lax.psum_scatter(term.astype(BF16), AXES, scatter_dimension=0, tiled=True)


def on_device(
    tokens,
    segment_ids,
    w_qkv,
    qv_bias,
    w_out,
    out_bias,
    w_in,
    in_bias,
    w_back,
    back_bias,
    norm_gains,
    norm_shifts,
    out_cotangent,
    *,
    dp_size,
    head_size,
):
    micro, local, width = tokens.shape
    seq_len = segment_ids.shape[2]
    own_rows = local // seq_len
    part, own_width = w_qkv.shape[1], w_qkv.shape[2]
    shard = (3, part, own_width)

    gathered = lax.all_gather(w_qkv.reshape(3 * part, own_width), AXES, axis=0, tiled=True)
    qkv_full = (
        gathered.reshape((dp_size, head_size) + shard)
        .transpose(2, 0, 3, 1, 4)
        .reshape(3, dp_size * part, head_size * own_width)
    )
    out_full = gather(w_out.T)
    in_full = gather(w_in.T)
    back_full = gather(w_back.T)

    x = tokens.reshape(micro * local, width)
    segments = lax.dynamic_slice_in_dim(
        segment_ids, lax.axis_index("head") * own_rows, own_rows, 1
    ).reshape(micro * own_rows, seq_len)
    bias = jnp.stack([qv_bias[0], jnp.zeros_like(qv_bias[0]), qv_bias[1]])[:, None, :]
    qkv = (
        jnp.einsum("td,cdf->ctf", x, qkv_full, preferred_element_type=F32) + bias
    ).astype(BF16)
    context, totals = attend(segments, qkv)
    attended = dot(context, out_full, 1, 1) + out_bias
    normal_one, inverse_one = norm_stats(x.astype(F32) + attended)
    hidden = normal_one * norm_gains[0] + norm_shifts[0]
    hidden_low = hidden.astype(BF16)
    pre_act = dot(hidden_low, in_full, 1, 1) + in_bias
    cumulative, along = gelu_parts(pre_act)
    activation = (pre_act * cumulative).astype(BF16)
    slope = cumulative + along
    branch = dot(activation, back_full, 1, 1) + back_bias
    normal_two, inverse_two = norm_stats(hidden + branch)
    out = (normal_two * norm_gains[1] + norm_shifts[1]).astype(BF16)

    error = out_cotangent.reshape(micro * local, width).astype(F32)
    grad_two = norm_back(normal_two, inverse_two, error, norm_gains[1])
    gain_two = jnp.sum(error * normal_two, axis=0)
    shift_two = jnp.sum(error, axis=0)
    grad_branch = grad_two.astype(BF16)
    back_grad = reduce_rows(dot(grad_branch, activation, 0, 0))
    grad_pre = (slope * dot(grad_branch, back_full, 1, 0)).astype(BF16)
    in_grad = reduce_rows(dot(grad_pre, hidden_low, 0, 0))
    grad_hidden = grad_two + dot(grad_pre, in_full, 1, 0)
    grad_one = norm_back(normal_one, inverse_one, grad_hidden, norm_gains[0])
    gain_one = jnp.sum(grad_hidden * normal_one, axis=0)
    shift_one = jnp.sum(grad_hidden, axis=0)
    grad_attn = grad_one.astype(BF16)
    out_grad = reduce_rows(dot(grad_attn, context, 0, 0))
    grad_context = dot(grad_attn, out_full, 1, 0).astype(BF16)
    grad_qkv = attend_back(segments, qkv, totals, grad_context)
    term = jnp.einsum("td,ctf->cdf", x, grad_qkv, preferred_element_type=F32)
    term = (
        term.astype(BF16)
        .reshape(3, dp_size, part, head_size, own_width)
        .transpose(1, 3, 0, 2, 4)
        .reshape(dp_size * head_size * 3 * part, own_width)
    )
    qkv_grad = lax.psum_scatter(term, AXES, scatter_dimension=0, tiled=True)
    x_grad = grad_one + jnp.einsum(
        "ctf,cdf->td", grad_qkv, qkv_full, preferred_element_type=F32
    )
    small = jnp.concatenate(
        [
            jnp.sum(grad_qkv[0].astype(F32), axis=0),
            jnp.sum(grad_qkv[2].astype(F32), axis=0),
            jnp.sum(grad_attn.astype(F32), axis=0),
            jnp.sum(grad_pre.astype(F32), axis=0),
            jnp.sum(grad_branch.astype(F32), axis=0),
            gain_one,
            gain_two,
            shift_one,
            shift_two,
        ]
    )
    small = lax.psum(small, AXES)
    hidden_width = in_bias.shape[0]
    cuts, at = [], 0
    for size in (2 * width, width, hidden_width, width, 2 * width, 2 * width):
        cuts.append(small[at : at + size])
        at += size
    return (
        out.reshape(tokens.shape),
        x_grad.reshape(tokens.shape),
        qkv_grad.astype(F32).reshape(shard),
        cuts[0].reshape(2, width),
        out_grad.astype(F32).T,
        cuts[1],
        in_grad.astype(F32).T,
        cuts[2],
        back_grad.astype(F32).T,
        cuts[3],
        cuts[4].reshape(2, width),
        cuts[5].reshape(2, width),
    )


def solution(mesh):
    return jax.shard_map(
        functools.partial(
            on_device, dp_size=mesh.shape["dp"], head_size=mesh.shape["head"]
        ),
        mesh=mesh,
        in_specs=(
            P(None, AXES, None),
            P(None, "dp", None),
            P(None, "dp", "head"),
            P(),
            P(None, AXES),
            P(),
            P(None, AXES),
            P(),
            P(None, AXES),
            P(),
            P(),
            P(),
            P(None, AXES, None),
        ),
        out_specs=(
            P(None, AXES, None),
            P(None, AXES, None),
            P(None, "dp", "head"),
            P(),
            P(None, AXES),
            P(),
            P(None, AXES),
            P(),
            P(None, AXES),
            P(),
            P(),
            P(),
        ),
        check_vma=False,
    )
```

```python
import functools
import math

import jax
import jax.numpy as jnp
from jax import lax
from jax.experimental import pallas as pl
from jax.experimental.pallas import tpu as pltpu
from jax.sharding import PartitionSpec as P

HD = 64
NORM_EPS = 1e-05
MASKED = -1e30
AXES = ("dp", "head")
F32 = jnp.float32
BF16 = jnp.bfloat16
MESH = pl.DeviceIdType.MESH


def dot(left, right, left_dim, right_dim):
    return lax.dot_general(
        left, right, (((left_dim,), (right_dim,)), ((), ())), preferred_element_type=F32
    )


def fill_mask(segment_row, segment_col, mask_ref):
    @pl.when(pl.program_id(1) == 0)
    def _():
        mask_ref[...] = jnp.where(segment_col[0] == segment_row[0], 0.0, MASKED)


def lane_halves(rows):
    lane = lax.broadcasted_iota(jnp.int32, (rows, 2 * HD), 1)
    return lane < HD


def attend_kernel(seg_row, seg_col, qkv_ref, context_ref, total_ref, mask_ref):
    fill_mask(seg_row, seg_col, mask_ref)
    queries = qkv_ref[0] * jnp.asarray(HD**-0.5, BF16)
    key_rows = qkv_ref[1]
    values = qkv_ref[2]
    first = lane_halves(key_rows.shape[0])
    parts = []
    for head in range(2):
        keys_own = jnp.where(first if head == 0 else ~first, key_rows, jnp.zeros_like(key_rows))
        scores = dot(keys_own, queries, 1, 1) + mask_ref[...]
        highest = jnp.max(scores, axis=0, keepdims=True)
        exponent = jnp.exp(scores - highest)
        totals = jnp.sum(exponent, axis=0, keepdims=True)
        low = (exponent * (1.0 / totals)).astype(BF16)
        total_ref[0, 0, head : head + 1, :] = highest + jnp.log(totals)
        parts.append(dot(values, low, 0, 0))
    joined = jnp.concatenate([parts[0][:HD], parts[1][HD:]], axis=0)
    context_ref[...] = joined.T.astype(BF16)


def attend_back_kernel(seg_row, seg_col, qkv_ref, total_ref, grad_ref, out_ref, mask_ref):
    fill_mask(seg_row, seg_col, mask_ref)
    scale = jnp.asarray(HD**-0.5, BF16)
    queries = qkv_ref[0] * scale
    key_rows = qkv_ref[1]
    key_scaled = key_rows * scale
    values = qkv_ref[2]
    grad = grad_ref[...]
    first = lane_halves(key_rows.shape[0])
    grad_queries, grad_keys, grad_values = [], [], []
    for head in range(2):
        own = first if head == 0 else ~first
        zero = jnp.zeros_like(key_rows)
        scores = dot(jnp.where(own, key_rows, zero), queries, 1, 1) + mask_ref[...]
        probs = jnp.exp(scores - total_ref[0, 0, head : head + 1, :])
        grad_probs = dot(jnp.where(own, values, zero), grad, 1, 1)
        weighted = jnp.sum(probs * grad_probs, axis=0, keepdims=True)
        grad_scores = (probs * (grad_probs - weighted)).astype(BF16)
        grad_values.append(dot(probs.astype(BF16), grad, 1, 0))
        grad_keys.append(dot(grad_scores, queries, 1, 0))
        grad_queries.append(dot(key_scaled, grad_scores, 0, 0))
    joined = jnp.concatenate([grad_queries[0][:HD], grad_queries[1][HD:]], axis=0)
    out_ref[0] = joined.T.astype(BF16)
    out_ref[1] = jnp.where(first, grad_keys[0], grad_keys[1]).astype(BF16)
    out_ref[2] = jnp.where(first, grad_values[0], grad_values[1]).astype(BF16)


def attention_specs(seq_len):
    return dict(
        row=pl.BlockSpec((1, 1, seq_len), lambda r, h: (r, 0, 0)),
        col=pl.BlockSpec((1, seq_len, 1), lambda r, h: (r, 0, 0)),
        three=pl.BlockSpec((3, seq_len, 2 * HD), lambda r, h: (0, r, h)),
        one=pl.BlockSpec((seq_len, 2 * HD), lambda r, h: (r, h)),
        total=pl.BlockSpec((1, 1, 8, seq_len), lambda r, h: (r, h, 0, 0)),
    )


def attend(segments, qkv):
    rows, seq_len = segments.shape
    pairs = qkv.shape[2] // (2 * HD)
    s = attention_specs(seq_len)
    area = rows * pairs * 2 * seq_len * seq_len
    return pl.pallas_call(
        attend_kernel,
        grid=(rows, pairs),
        in_specs=[s["row"], s["col"], s["three"]],
        out_specs=[s["one"], s["total"]],
        out_shape=[
            jax.ShapeDtypeStruct(qkv.shape[1:], BF16),
            jax.ShapeDtypeStruct((rows, pairs, 8, seq_len), F32),
        ],
        scratch_shapes=[pltpu.VMEM((seq_len, seq_len), F32)],
        cost_estimate=pl.CostEstimate(
            flops=area * 512, bytes_accessed=qkv.size * 3, transcendentals=area
        ),
        name="attend",
    )(segments[:, None, :], segments[:, :, None], qkv)


def attend_back(segments, qkv, totals, grad):
    rows, seq_len = segments.shape
    pairs = qkv.shape[2] // (2 * HD)
    s = attention_specs(seq_len)
    area = rows * pairs * 2 * seq_len * seq_len
    return pl.pallas_call(
        attend_back_kernel,
        grid=(rows, pairs),
        in_specs=[s["row"], s["col"], s["three"], s["total"], s["one"]],
        out_specs=s["three"],
        out_shape=jax.ShapeDtypeStruct(qkv.shape, BF16),
        scratch_shapes=[pltpu.VMEM((seq_len, seq_len), F32)],
        cost_estimate=pl.CostEstimate(
            flops=area * 1280, bytes_accessed=qkv.size * 5, transcendentals=area
        ),
        name="attend_back",
    )(segments[:, None, :], segments[:, :, None], qkv, totals, grad)


def gelu_parts(value):
    size = jnp.abs(value)
    bell = jnp.exp(-0.5 * value * value)
    t = 1.0 / (1.0 + (0.3275911 / math.sqrt(2.0)) * size)
    series = 1.061405429 / 2
    for factor in (-1.453152027 / 2, 1.421413741 / 2, -0.284496736 / 2, 0.254829592 / 2):
        series = series * t + factor
    tail = series * t * bell
    cumulative = jnp.where(value < 0, tail, 1.0 - tail)
    return cumulative, value * bell * (1.0 / math.sqrt(2.0 * math.pi))


def norm_stats(residual):
    average = jnp.mean(residual, axis=-1, keepdims=True)
    centred = residual - average
    spread = jnp.mean(centred * centred, axis=-1, keepdims=True)
    inverse = lax.rsqrt(spread + NORM_EPS)
    return centred * inverse, inverse


def norm_back(normal, inverse, grad, gain):
    weighted = grad * gain
    along = jnp.mean(weighted * normal, axis=-1, keepdims=True)
    return inverse * (weighted - jnp.mean(weighted, axis=-1, keepdims=True) - normal * along)


def sum_kernel(sizes, x_ref, out_ref, held, arrived, send_sem, recv_sem):
    partners = []
    for axis, size in sizes:
        index = lax.axis_index(axis)
        bit = 1
        while bit < size:
            partners.append({axis: index + bit - 2 * bit * ((index // bit) % 2)})
            bit *= 2
    barrier = pltpu.get_barrier_semaphore()
    for partner in partners:
        pl.semaphore_signal(barrier, 1, device_id=partner, device_id_type=MESH)
    pl.semaphore_wait(barrier, len(partners))
    held[0] = x_ref[...]
    for step, partner in enumerate(partners):
        copy = pltpu.make_async_remote_copy(
            src_ref=held.at[step],
            dst_ref=arrived.at[step],
            send_sem=send_sem.at[step],
            recv_sem=recv_sem.at[step],
            device_id=partner,
            device_id_type=MESH,
        )
        copy.start()
        copy.wait()
        held[step + 1] = held[step] + arrived[step]
    out_ref[...] = held[len(partners)]


def sum_everywhere(x, sizes):
    steps = sum(size.bit_length() - 1 for _, size in sizes)
    return pl.pallas_call(
        functools.partial(sum_kernel, sizes),
        out_shape=jax.ShapeDtypeStruct(x.shape, x.dtype),
        in_specs=[pl.BlockSpec(memory_space=pltpu.VMEM)],
        out_specs=pl.BlockSpec(memory_space=pltpu.VMEM),
        scratch_shapes=[
            pltpu.VMEM((steps + 1,) + x.shape, x.dtype),
            pltpu.VMEM((steps,) + x.shape, x.dtype),
            pltpu.SemaphoreType.DMA((steps,)),
            pltpu.SemaphoreType.DMA((steps,)),
        ],
        compiler_params=pltpu.CompilerParams(collective_id=0, has_side_effects=True),
        name="sum_everywhere",
    )(x)


def on_device(
    tokens,
    segment_ids,
    w_qkv,
    qv_bias,
    w_out,
    out_bias,
    w_in,
    in_bias,
    w_back,
    back_bias,
    norm_gains,
    norm_shifts,
    out_cotangent,
    *,
    dp_size,
    head_size,
):
    micro, local, width = tokens.shape
    seq_len = segment_ids.shape[2]
    own_rows = local // seq_len
    part, own_width = w_qkv.shape[1], w_qkv.shape[2]
    shard = (3, part, own_width)

    devices = dp_size * head_size
    hidden_width = in_bias.shape[0]
    out_part, in_part = width // devices, hidden_width // devices
    chunks = hidden_width // width
    back_part = chunks * out_part
    qkv_part = 3 * part * own_width // width
    packed = jnp.concatenate(
        [
            w_in.T,
            w_back.reshape(chunks, width, out_part).transpose(0, 2, 1).reshape(back_part, width),
            w_qkv.reshape(qkv_part, width),
            w_out.T,
        ]
    )
    gathered = lax.all_gather(packed, AXES, axis=0, tiled=False)
    marks = (0, in_part, in_part + back_part, in_part + back_part + qkv_part)
    in_full = gathered[:, : marks[1]].reshape(hidden_width, width)
    back_full = (
        gathered[:, marks[1] : marks[2]]
        .reshape(devices, chunks, out_part, width)
        .transpose(0, 2, 1, 3)
        .reshape(width, hidden_width)
    )
    qkv_full = (
        gathered[:, marks[2] : marks[3]]
        .reshape((dp_size, head_size) + shard)
        .transpose(2, 0, 3, 1, 4)
        .reshape(3, dp_size * part, head_size * own_width)
    )
    out_full = gathered[:, marks[3] :].reshape(width, width)

    x = tokens.reshape(micro * local, width)
    segments = lax.dynamic_slice_in_dim(
        segment_ids, lax.axis_index("head") * own_rows, own_rows, 1
    ).reshape(micro * own_rows, seq_len)
    bias = jnp.stack([qv_bias[0], jnp.zeros_like(qv_bias[0]), qv_bias[1]])[:, None, :]
    qkv = (
        jnp.einsum("td,cdf->ctf", x, qkv_full, preferred_element_type=F32) + bias
    ).astype(BF16)
    context, totals = attend(segments, qkv)
    attended = dot(context, out_full, 1, 1) + out_bias
    normal_one, inverse_one = norm_stats(x.astype(F32) + attended)
    hidden = normal_one * norm_gains[0] + norm_shifts[0]
    hidden_low = hidden.astype(BF16)
    pre_act = dot(hidden_low, in_full, 1, 1) + in_bias
    cumulative, along = gelu_parts(pre_act)
    activation = (pre_act * cumulative).astype(BF16)
    slope = cumulative + along
    branch = dot(activation, back_full, 1, 1) + back_bias
    normal_two, inverse_two = norm_stats(hidden + branch)
    out = (normal_two * norm_gains[1] + norm_shifts[1]).astype(BF16)

    error = out_cotangent.reshape(micro * local, width).astype(F32)
    grad_two = norm_back(normal_two, inverse_two, error, norm_gains[1])
    gain_two = jnp.sum(error * normal_two, axis=0)
    shift_two = jnp.sum(error, axis=0)
    grad_branch = grad_two.astype(BF16)
    back_term = dot(grad_branch, activation, 0, 0).astype(BF16)
    grad_pre = (slope * dot(grad_branch, back_full, 1, 0)).astype(BF16)
    in_term = dot(grad_pre, hidden_low, 0, 0).astype(BF16)
    grad_hidden = grad_two + dot(grad_pre, in_full, 1, 0)
    grad_one = norm_back(normal_one, inverse_one, grad_hidden, norm_gains[0])
    gain_one = jnp.sum(grad_hidden * normal_one, axis=0)
    shift_one = jnp.sum(grad_hidden, axis=0)
    grad_attn = grad_one.astype(BF16)
    out_term = dot(grad_attn, context, 0, 0).astype(BF16)
    grad_context = dot(grad_attn, out_full, 1, 0).astype(BF16)
    grad_qkv = attend_back(segments, qkv, totals, grad_context)
    term = jnp.einsum("td,ctf->cdf", x, grad_qkv, preferred_element_type=F32)
    term = (
        term.astype(BF16)
        .reshape(3, dp_size, part, head_size, own_width)
        .transpose(1, 3, 0, 2, 4)
        .reshape(devices, qkv_part, width)
    )
    back_term = (
        back_term.reshape(devices, out_part, chunks, width)
        .transpose(0, 2, 1, 3)
        .reshape(devices, back_part, width)
    )
    terms = jnp.concatenate(
        [
            in_term.reshape(devices, in_part, width),
            back_term,
            term,
            out_term.reshape(devices, out_part, width),
        ],
        axis=1,
    )
    summed = lax.psum_scatter(terms, AXES, scatter_dimension=0, tiled=False).astype(F32)
    x_grad = grad_one + jnp.einsum(
        "ctf,cdf->td", grad_qkv, qkv_full, preferred_element_type=F32
    )
    small = jnp.concatenate(
        [
            jnp.sum(grad_qkv[0].astype(F32), axis=0),
            jnp.sum(grad_qkv[2].astype(F32), axis=0),
            jnp.sum(grad_attn.astype(F32), axis=0),
            jnp.sum(grad_pre.astype(F32), axis=0),
            jnp.sum(grad_branch.astype(F32), axis=0),
            gain_one,
            gain_two,
            shift_one,
            shift_two,
        ]
    )
    small = sum_everywhere(
        small.reshape(-1, 128), (("dp", dp_size), ("head", head_size))
    ).reshape(-1)
    cuts, at = [], 0
    for size in (2 * width, width, hidden_width, width, 2 * width, 2 * width):
        cuts.append(small[at : at + size])
        at += size
    return (
        out.reshape(tokens.shape),
        x_grad.reshape(tokens.shape),
        summed[marks[2] : marks[3]].reshape(shard),
        cuts[0].reshape(2, width),
        summed[marks[3] :].T,
        cuts[1],
        summed[: marks[1]].T,
        cuts[2],
        summed[marks[1] : marks[2]]
        .reshape(chunks, out_part, width)
        .transpose(0, 2, 1)
        .reshape(hidden_width, out_part),
        cuts[3],
        cuts[4].reshape(2, width),
        cuts[5].reshape(2, width),
    )


def solution(mesh):
    return jax.shard_map(
        functools.partial(
            on_device, dp_size=mesh.shape["dp"], head_size=mesh.shape["head"]
        ),
        mesh=mesh,
        in_specs=(
            P(None, AXES, None),
            P(None, "dp", None),
            P(None, "dp", "head"),
            P(),
            P(None, AXES),
            P(),
            P(None, AXES),
            P(),
            P(None, AXES),
            P(),
            P(),
            P(),
            P(None, AXES, None),
        ),
        out_specs=(
            P(None, AXES, None),
            P(None, AXES, None),
            P(None, "dp", "head"),
            P(),
            P(None, AXES),
            P(),
            P(None, AXES),
            P(),
            P(None, AXES),
            P(),
            P(),
            P(),
        ),
        check_vma=False,
    )
```

```python
import functools
import math

import jax
import jax.numpy as jnp
from jax import lax
from jax.experimental import pallas as pl
from jax.experimental.pallas import tpu as pltpu
from jax.sharding import PartitionSpec as P

HD = 64
NORM_EPS = 1e-05
MASKED = -1e30
AXES = ("dp", "head")
F32 = jnp.float32
BF16 = jnp.bfloat16
MESH = pl.DeviceIdType.MESH


def dot(left, right, left_dim, right_dim):
    return lax.dot_general(
        left, right, (((left_dim,), (right_dim,)), ((), ())), preferred_element_type=F32
    )


def fill_mask(segment_row, segment_col, mask_ref):
    @pl.when(pl.program_id(1) == 0)
    def _():
        mask_ref[...] = jnp.where(segment_col[0] == segment_row[0], 0.0, MASKED)


def lane_halves(rows):
    lane = lax.broadcasted_iota(jnp.int32, (rows, 2 * HD), 1)
    return lane < HD


def attend_kernel(seg_row, seg_col, qkv_ref, context_ref, total_ref, mask_ref):
    fill_mask(seg_row, seg_col, mask_ref)
    queries = qkv_ref[0] * jnp.asarray(HD**-0.5, BF16)
    key_rows = qkv_ref[1]
    values = qkv_ref[2]
    first = lane_halves(key_rows.shape[0])
    parts = []
    for head in range(2):
        keys_own = jnp.where(first if head == 0 else ~first, key_rows, jnp.zeros_like(key_rows))
        scores = dot(keys_own, queries, 1, 1) + mask_ref[...]
        highest = jnp.max(scores, axis=0, keepdims=True)
        exponent = jnp.exp(scores - highest)
        totals = jnp.sum(exponent, axis=0, keepdims=True)
        low = (exponent * (1.0 / totals)).astype(BF16)
        total_ref[0, 0, head : head + 1, :] = highest + jnp.log(totals)
        parts.append(dot(values, low, 0, 0))
    joined = jnp.concatenate([parts[0][:HD], parts[1][HD:]], axis=0)
    context_ref[...] = joined.T.astype(BF16)


def attend_back_kernel(seg_row, seg_col, qkv_ref, total_ref, grad_ref, out_ref, mask_ref):
    fill_mask(seg_row, seg_col, mask_ref)
    scale = jnp.asarray(HD**-0.5, BF16)
    queries = qkv_ref[0] * scale
    key_rows = qkv_ref[1]
    key_scaled = key_rows * scale
    values = qkv_ref[2]
    grad = grad_ref[...]
    first = lane_halves(key_rows.shape[0])
    grad_queries, grad_keys, grad_values = [], [], []
    for head in range(2):
        own = first if head == 0 else ~first
        zero = jnp.zeros_like(key_rows)
        scores = dot(jnp.where(own, key_rows, zero), queries, 1, 1) + mask_ref[...]
        probs = jnp.exp(scores - total_ref[0, 0, head : head + 1, :])
        grad_probs = dot(jnp.where(own, values, zero), grad, 1, 1)
        weighted = jnp.sum(probs * grad_probs, axis=0, keepdims=True)
        grad_scores = (probs * (grad_probs - weighted)).astype(BF16)
        grad_values.append(dot(probs.astype(BF16), grad, 1, 0))
        grad_keys.append(dot(grad_scores, queries, 1, 0))
        grad_queries.append(dot(key_scaled, grad_scores, 0, 0))
    joined = jnp.concatenate([grad_queries[0][:HD], grad_queries[1][HD:]], axis=0)
    out_ref[0] = joined.T.astype(BF16)
    out_ref[1] = jnp.where(first, grad_keys[0], grad_keys[1]).astype(BF16)
    out_ref[2] = jnp.where(first, grad_values[0], grad_values[1]).astype(BF16)


def attention_specs(seq_len):
    return dict(
        row=pl.BlockSpec((1, 1, seq_len), lambda r, h: (r, 0, 0)),
        col=pl.BlockSpec((1, seq_len, 1), lambda r, h: (r, 0, 0)),
        three=pl.BlockSpec((3, seq_len, 2 * HD), lambda r, h: (0, r, h)),
        one=pl.BlockSpec((seq_len, 2 * HD), lambda r, h: (r, h)),
        total=pl.BlockSpec((1, 1, 8, seq_len), lambda r, h: (r, h, 0, 0)),
    )


def attend(segments, qkv):
    rows, seq_len = segments.shape
    pairs = qkv.shape[2] // (2 * HD)
    s = attention_specs(seq_len)
    area = rows * pairs * 2 * seq_len * seq_len
    return pl.pallas_call(
        attend_kernel,
        grid=(rows, pairs),
        in_specs=[s["row"], s["col"], s["three"]],
        out_specs=[s["one"], s["total"]],
        out_shape=[
            jax.ShapeDtypeStruct(qkv.shape[1:], BF16),
            jax.ShapeDtypeStruct((rows, pairs, 8, seq_len), F32),
        ],
        scratch_shapes=[pltpu.VMEM((seq_len, seq_len), F32)],
        cost_estimate=pl.CostEstimate(
            flops=area * 512, bytes_accessed=qkv.size * 3, transcendentals=area
        ),
        name="attend",
    )(segments[:, None, :], segments[:, :, None], qkv)


def attend_back(segments, qkv, totals, grad):
    rows, seq_len = segments.shape
    pairs = qkv.shape[2] // (2 * HD)
    s = attention_specs(seq_len)
    area = rows * pairs * 2 * seq_len * seq_len
    return pl.pallas_call(
        attend_back_kernel,
        grid=(rows, pairs),
        in_specs=[s["row"], s["col"], s["three"], s["total"], s["one"]],
        out_specs=s["three"],
        out_shape=jax.ShapeDtypeStruct(qkv.shape, BF16),
        scratch_shapes=[pltpu.VMEM((seq_len, seq_len), F32)],
        cost_estimate=pl.CostEstimate(
            flops=area * 1280, bytes_accessed=qkv.size * 5, transcendentals=area
        ),
        name="attend_back",
    )(segments[:, None, :], segments[:, :, None], qkv, totals, grad)


def gelu_parts(value):
    size = jnp.abs(value)
    bell = jnp.exp(-0.5 * value * value)
    t = 1.0 / (1.0 + (0.3275911 / math.sqrt(2.0)) * size)
    series = 1.061405429 / 2
    for factor in (-1.453152027 / 2, 1.421413741 / 2, -0.284496736 / 2, 0.254829592 / 2):
        series = series * t + factor
    tail = series * t * bell
    cumulative = jnp.where(value < 0, tail, 1.0 - tail)
    return cumulative, value * bell * (1.0 / math.sqrt(2.0 * math.pi))


def norm_stats(residual):
    average = jnp.mean(residual, axis=-1, keepdims=True)
    centred = residual - average
    spread = jnp.mean(centred * centred, axis=-1, keepdims=True)
    inverse = lax.rsqrt(spread + NORM_EPS)
    return centred * inverse, inverse


def norm_back(normal, inverse, grad, gain):
    weighted = grad * gain
    along = jnp.mean(weighted * normal, axis=-1, keepdims=True)
    return inverse * (weighted - jnp.mean(weighted, axis=-1, keepdims=True) - normal * along)


def sum_kernel(sizes, x_ref, out_ref, held, arrived, send_sem, recv_sem):
    partners = []
    for axis, size in sizes:
        index = lax.axis_index(axis)
        bit = 1
        while bit < size:
            partners.append({axis: index + bit - 2 * bit * ((index // bit) % 2)})
            bit *= 2
    barrier = pltpu.get_barrier_semaphore()
    for partner in partners:
        pl.semaphore_signal(barrier, 1, device_id=partner, device_id_type=MESH)
    pl.semaphore_wait(barrier, len(partners))
    held[0] = x_ref[...]
    for step, partner in enumerate(partners):
        copy = pltpu.make_async_remote_copy(
            src_ref=held.at[step],
            dst_ref=arrived.at[step],
            send_sem=send_sem.at[step],
            recv_sem=recv_sem.at[step],
            device_id=partner,
            device_id_type=MESH,
        )
        copy.start()
        copy.wait()
        held[step + 1] = held[step] + arrived[step]
    out_ref[...] = held[len(partners)]


def exchange_orders(dp_size):
    bits = list(range(dp_size.bit_length() - 2, -1, -1))
    return bits[:-1] + ["head", bits[-1]], bits[:-2] + ["head", bits[-2], bits[-1]]


def own_bit(bit):
    return lax.axis_index("head") if bit == "head" else (lax.axis_index("dp") // 2**bit) % 2


def partner_of(bit):
    index = lax.axis_index("head" if bit == "head" else "dp")
    step = 1 if bit == "head" else 2**bit
    return {"head" if bit == "head" else "dp": index + step - 2 * step * own_bit(bit)}


def meet(bits):
    barrier = pltpu.get_barrier_semaphore()
    for bit in bits:
        pl.semaphore_signal(barrier, 1, device_id=partner_of(bit), device_id_type=MESH)
    pl.semaphore_wait(barrier, len(bits))


def lanes_of(half, width):
    return pl.ds(pl.multiple_of(half * width, width), width)


def gather_kernel(dp_size, qkv_ref, out_ref, qkv_full, out_full, own_sem, send_sem, recv_sem):
    orders = exchange_orders(dp_size)
    bits = [bit for bit in orders[0] if bit != "head"]
    width = qkv_ref.shape[2]
    meet(orders[0])

    def qkv_view(kinds, done):
        index = tuple(slice(None) if bit in done else own_bit(bit) for bit in bits)
        lanes = slice(None) if "head" in done else lanes_of(own_bit("head"), width)
        return qkv_full.at[(kinds,) + index + (slice(None), lanes)]

    def out_view(done):
        return out_full.at[
            tuple(slice(None) if bit in done else own_bit(bit) for bit in bits + ["head"])
        ]

    own = [
        pltpu.make_async_copy(qkv_ref, qkv_view(slice(None), ()), own_sem.at[0]),
        pltpu.make_async_copy(out_ref, out_view(()), own_sem.at[1]),
    ]
    for copy in own:
        copy.start()
    for copy in own:
        copy.wait()
    for step in range(len(orders[0])):
        copies = []
        for stream in range(3):
            order = orders[0] if stream == 0 else orders[1]
            done = order[:step]
            if stream == 2:
                view = out_view(done)
            else:
                view = qkv_view(slice(0, 2) if stream == 0 else slice(2, 3), done)
            copies.append(
                pltpu.make_async_remote_copy(
                    src_ref=view,
                    dst_ref=view,
                    send_sem=send_sem.at[step, stream],
                    recv_sem=recv_sem.at[step, stream],
                    device_id=partner_of(order[step]),
                    device_id_type=MESH,
                )
            )
        for copy in copies:
            copy.start()
        for copy in copies:
            copy.wait()


def gather_projections(qkv_shard, out_shard, dp_size):
    _, part, own_width = qkv_shard.shape
    bits = (2,) * (dp_size.bit_length() - 1)
    steps = len(bits) + 1
    vmem = pl.BlockSpec(memory_space=pltpu.VMEM)
    qkv_full, out_full = pl.pallas_call(
        functools.partial(gather_kernel, dp_size),
        out_shape=[
            jax.ShapeDtypeStruct((3,) + bits + (part, 2 * own_width), BF16),
            jax.ShapeDtypeStruct(bits + (2,) + out_shard.shape, BF16),
        ],
        in_specs=[vmem, vmem],
        out_specs=[vmem, vmem],
        scratch_shapes=[
            pltpu.SemaphoreType.DMA((2,)),
            pltpu.SemaphoreType.DMA((steps, 3)),
            pltpu.SemaphoreType.DMA((steps, 3)),
        ],
        compiler_params=pltpu.CompilerParams(collective_id=1, has_side_effects=True),
        cost_estimate=pl.CostEstimate(flops=0, bytes_accessed=2**27, transcendentals=0),
        name="gather_projections",
    )(qkv_shard, out_shard)
    return (
        qkv_full.reshape(3, dp_size * part, 2 * own_width),
        out_full.reshape(dp_size * 2 * out_shard.shape[0], out_shard.shape[1]),
    )


def reduce_kernel(dp_size, qkv_ref, out_ref, qkv_sum, out_sum, *scratch):
    steps = len(exchange_orders(dp_size)[0])
    arrived, held = scratch[: 3 * steps], scratch[3 * steps : -2]
    send_sem, recv_sem = scratch[-2:]
    orders = [list(reversed(order)) for order in exchange_orders(dp_size)]
    meet(orders[0])
    bits = [bit for bit in orders[0] if bit != "head"]
    bits.sort(reverse=True)
    width = qkv_sum.shape[2]

    def view(ref, kinds, done, bit, half):
        index = tuple(half if b == bit else slice(None) for b in bits if b not in done)
        if kinds is None:
            if "head" not in done:
                index += (half if bit == "head" else slice(None),)
            return index
        lanes = lanes_of(half, width) if bit == "head" else slice(None)
        return (kinds,) + index + (slice(None), lanes)

    for step in range(steps):
        copies, mine = [], []
        for stream in range(3):
            order = orders[0] if stream == 0 else orders[1]
            bit, done = order[step], order[:step]
            if step == 0:
                source = out_ref if stream == 2 else qkv_ref
                kinds = (slice(0, 2), slice(2, 3), None)[stream]
            else:
                source = held[3 * (step - 1) + stream]
                kinds = None if stream == 2 else slice(None)
            target = arrived[3 * step + stream]
            copies.append(
                pltpu.make_async_remote_copy(
                    src_ref=source.at[view(source, kinds, done, bit, 1 - own_bit(bit))],
                    dst_ref=target,
                    send_sem=send_sem.at[step, stream],
                    recv_sem=recv_sem.at[step, stream],
                    device_id=partner_of(bit),
                    device_id_type=MESH,
                )
            )
            mine.append((source, view(source, kinds, done, bit, own_bit(bit)), target))
        for copy in copies:
            copy.start()
        for stream in range(3):
            copies[stream].wait()
            source, index, target = mine[stream]
            total = source[index].astype(F32) + target[...].astype(F32)
            if step < steps - 1:
                held[3 * step + stream][...] = total.astype(BF16)
            elif stream == 2:
                out_sum[...] = total
            elif stream == 0:
                qkv_sum[0:2] = total
            else:
                qkv_sum[2:3] = total


def reduce_projections(qkv_term, out_term, dp_size):
    count = dp_size.bit_length() - 1
    part, own_width = qkv_term.shape[1] // dp_size, qkv_term.shape[2] // 2
    out_part = out_term.shape[0] // (2 * dp_size)
    orders = [list(reversed(order)) for order in exchange_orders(dp_size)]
    shapes = []
    for step in range(count + 1):
        for stream in range(3):
            done = orders[0 if stream == 0 else 1][: step + 1]
            left = (2,) * (count - sum(bit != "head" for bit in done))
            if stream == 2:
                head = () if "head" in done else (2,)
                shapes.append(left + head + (out_part, out_term.shape[1]))
            else:
                wide = own_width if "head" in done else 2 * own_width
                shapes.append(((2, 1)[stream],) + left + (part, wide))
    vmem = pl.BlockSpec(memory_space=pltpu.VMEM)
    buffers = [pltpu.VMEM(shape, BF16) for shape in shapes]
    return pl.pallas_call(
        functools.partial(reduce_kernel, dp_size),
        out_shape=[
            jax.ShapeDtypeStruct((3, part, own_width), F32),
            jax.ShapeDtypeStruct((out_part, out_term.shape[1]), F32),
        ],
        in_specs=[vmem, vmem],
        out_specs=[vmem, vmem],
        scratch_shapes=buffers
        + buffers[: 3 * count]
        + [pltpu.SemaphoreType.DMA((count + 1, 3)), pltpu.SemaphoreType.DMA((count + 1, 3))],
        compiler_params=pltpu.CompilerParams(collective_id=2, has_side_effects=True),
        cost_estimate=pl.CostEstimate(flops=0, bytes_accessed=2**27, transcendentals=0),
        name="reduce_projections",
    )(
        qkv_term.reshape((3,) + (2,) * count + (part, 2 * own_width)),
        out_term.reshape((2,) * (count + 1) + (out_part, out_term.shape[1])),
    )


def sum_everywhere(x, sizes):
    steps = sum(size.bit_length() - 1 for _, size in sizes)
    return pl.pallas_call(
        functools.partial(sum_kernel, sizes),
        out_shape=jax.ShapeDtypeStruct(x.shape, x.dtype),
        in_specs=[pl.BlockSpec(memory_space=pltpu.VMEM)],
        out_specs=pl.BlockSpec(memory_space=pltpu.VMEM),
        scratch_shapes=[
            pltpu.VMEM((steps + 1,) + x.shape, x.dtype),
            pltpu.VMEM((steps,) + x.shape, x.dtype),
            pltpu.SemaphoreType.DMA((steps,)),
            pltpu.SemaphoreType.DMA((steps,)),
        ],
        compiler_params=pltpu.CompilerParams(collective_id=0, has_side_effects=True),
        name="sum_everywhere",
    )(x)


def on_device(
    tokens,
    segment_ids,
    w_qkv,
    qv_bias,
    w_out,
    out_bias,
    w_in,
    in_bias,
    w_back,
    back_bias,
    norm_gains,
    norm_shifts,
    out_cotangent,
    *,
    dp_size,
    head_size,
):
    micro, local, width = tokens.shape
    seq_len = segment_ids.shape[2]
    own_rows = local // seq_len

    devices = dp_size * head_size
    hidden_width = in_bias.shape[0]
    out_part, in_part = width // devices, hidden_width // devices
    chunks = hidden_width // width
    back_part = chunks * out_part
    packed = jnp.concatenate(
        [
            w_in.T,
            w_back.reshape(chunks, width, out_part).transpose(0, 2, 1).reshape(back_part, width),
        ]
    )
    gathered = lax.all_gather(packed, AXES, axis=0, tiled=False)
    in_full = gathered[:, :in_part].reshape(hidden_width, width)
    back_full = (
        gathered[:, in_part:]
        .reshape(devices, chunks, out_part, width)
        .transpose(0, 2, 1, 3)
        .reshape(width, hidden_width)
    )
    qkv_full, out_full = gather_projections(w_qkv, w_out.T, dp_size)

    x = tokens.reshape(micro * local, width)
    segments = lax.dynamic_slice_in_dim(
        segment_ids, lax.axis_index("head") * own_rows, own_rows, 1
    ).reshape(micro * own_rows, seq_len)
    bias = jnp.stack([qv_bias[0], jnp.zeros_like(qv_bias[0]), qv_bias[1]])[:, None, :]
    qkv = (
        jnp.einsum("td,cdf->ctf", x, qkv_full, preferred_element_type=F32) + bias
    ).astype(BF16)
    context, totals = attend(segments, qkv)
    attended = dot(context, out_full, 1, 1) + out_bias
    normal_one, inverse_one = norm_stats(x.astype(F32) + attended)
    hidden = normal_one * norm_gains[0] + norm_shifts[0]
    hidden_low = hidden.astype(BF16)
    pre_act = dot(hidden_low, in_full, 1, 1) + in_bias
    cumulative, along = gelu_parts(pre_act)
    activation = (pre_act * cumulative).astype(BF16)
    slope = cumulative + along
    branch = dot(activation, back_full, 1, 1) + back_bias
    normal_two, inverse_two = norm_stats(hidden + branch)
    out = (normal_two * norm_gains[1] + norm_shifts[1]).astype(BF16)

    error = out_cotangent.reshape(micro * local, width).astype(F32)
    grad_two = norm_back(normal_two, inverse_two, error, norm_gains[1])
    gain_two = jnp.sum(error * normal_two, axis=0)
    shift_two = jnp.sum(error, axis=0)
    grad_branch = grad_two.astype(BF16)
    back_term = dot(grad_branch, activation, 0, 0).astype(BF16)
    grad_pre = (slope * dot(grad_branch, back_full, 1, 0)).astype(BF16)
    in_term = dot(grad_pre, hidden_low, 0, 0).astype(BF16)
    back_term = (
        back_term.reshape(devices, out_part, chunks, width)
        .transpose(0, 2, 1, 3)
        .reshape(devices, back_part, width)
    )
    terms = jnp.concatenate(
        [
            in_term.reshape(devices, in_part, width),
            back_term,
        ],
        axis=1,
    )
    summed = lax.psum_scatter(terms, AXES, scatter_dimension=0, tiled=False).astype(F32)
    grad_hidden = grad_two + dot(grad_pre, in_full, 1, 0)
    grad_one = norm_back(normal_one, inverse_one, grad_hidden, norm_gains[0])
    gain_one = jnp.sum(grad_hidden * normal_one, axis=0)
    shift_one = jnp.sum(grad_hidden, axis=0)
    grad_attn = grad_one.astype(BF16)
    out_term = dot(grad_attn, context, 0, 0).astype(BF16)
    grad_context = dot(grad_attn, out_full, 1, 0).astype(BF16)
    grad_qkv = attend_back(segments, qkv, totals, grad_context)
    term = jnp.einsum("td,ctf->cdf", x, grad_qkv, preferred_element_type=F32)
    qkv_grad, out_grad = reduce_projections(term.astype(BF16), out_term, dp_size)
    x_grad = grad_one + jnp.einsum(
        "ctf,cdf->td", grad_qkv, qkv_full, preferred_element_type=F32
    )
    small = jnp.concatenate(
        [
            jnp.sum(grad_qkv[0].astype(F32), axis=0),
            jnp.sum(grad_qkv[2].astype(F32), axis=0),
            jnp.sum(grad_attn.astype(F32), axis=0),
            jnp.sum(grad_pre.astype(F32), axis=0),
            jnp.sum(grad_branch.astype(F32), axis=0),
            gain_one,
            gain_two,
            shift_one,
            shift_two,
        ]
    )
    small = sum_everywhere(
        small.reshape(-1, 128), (("dp", dp_size), ("head", head_size))
    ).reshape(-1)
    cuts, at = [], 0
    for size in (2 * width, width, hidden_width, width, 2 * width, 2 * width):
        cuts.append(small[at : at + size])
        at += size
    return (
        out.reshape(tokens.shape),
        x_grad.reshape(tokens.shape),
        qkv_grad,
        cuts[0].reshape(2, width),
        out_grad.T,
        cuts[1],
        summed[:in_part].T,
        cuts[2],
        summed[in_part:]
        .reshape(chunks, out_part, width)
        .transpose(0, 2, 1)
        .reshape(hidden_width, out_part),
        cuts[3],
        cuts[4].reshape(2, width),
        cuts[5].reshape(2, width),
    )


def solution(mesh):
    return jax.shard_map(
        functools.partial(
            on_device, dp_size=mesh.shape["dp"], head_size=mesh.shape["head"]
        ),
        mesh=mesh,
        in_specs=(
            P(None, AXES, None),
            P(None, "dp", None),
            P(None, "dp", "head"),
            P(),
            P(None, AXES),
            P(),
            P(None, AXES),
            P(),
            P(None, AXES),
            P(),
            P(),
            P(),
            P(None, AXES, None),
        ),
        out_specs=(
            P(None, AXES, None),
            P(None, AXES, None),
            P(None, "dp", "head"),
            P(),
            P(None, AXES),
            P(),
            P(None, AXES),
            P(),
            P(None, AXES),
            P(),
            P(),
            P(),
        ),
        check_vma=False,
    )
```

```python
import functools
import math

import jax
import jax.numpy as jnp
from jax import lax
from jax.experimental import pallas as pl
from jax.experimental.pallas import tpu as pltpu
from jax.sharding import PartitionSpec as P

HD = 64
NORM_EPS = 1e-05
MASKED = -1e30
AXES = ("dp", "head")
F32 = jnp.float32
BF16 = jnp.bfloat16
MESH = pl.DeviceIdType.MESH
TILE = 256


def dot(left, right, left_dim, right_dim):
    return lax.dot_general(
        left, right, (((left_dim,), (right_dim,)), ((), ())), preferred_element_type=F32
    )


def fill_mask(segment_row, segment_col, mask_ref):
    @pl.when(pl.program_id(1) == 0)
    def _():
        mask_ref[...] = jnp.where(segment_col[0] == segment_row[0], 0.0, MASKED)


def lane_halves(rows):
    lane = lax.broadcasted_iota(jnp.int32, (rows, 2 * HD), 1)
    return lane < HD


def attend_kernel(seg_row, seg_col, qkv_ref, context_ref, total_ref, mask_ref):
    fill_mask(seg_row, seg_col, mask_ref)
    queries = qkv_ref[0] * jnp.asarray(HD**-0.5, BF16)
    key_rows = qkv_ref[1]
    values = qkv_ref[2]
    first = lane_halves(key_rows.shape[0])
    parts = []
    for head in range(2):
        keys_own = jnp.where(first if head == 0 else ~first, key_rows, jnp.zeros_like(key_rows))
        scores = dot(keys_own, queries, 1, 1) + mask_ref[...]
        highest = jnp.max(scores, axis=0, keepdims=True)
        exponent = jnp.exp(scores - highest)
        totals = jnp.sum(exponent, axis=0, keepdims=True)
        low = (exponent * (1.0 / totals)).astype(BF16)
        total_ref[0, 0, head : head + 1, :] = highest + jnp.log(totals)
        parts.append(dot(values, low, 0, 0))
    joined = jnp.concatenate([parts[0][:HD], parts[1][HD:]], axis=0)
    context_ref[...] = joined.T.astype(BF16)


def attend_back_kernel(seg_row, seg_col, qkv_ref, total_ref, grad_ref, out_ref, mask_ref):
    fill_mask(seg_row, seg_col, mask_ref)
    scale = jnp.asarray(HD**-0.5, BF16)
    queries = qkv_ref[0] * scale
    key_rows = qkv_ref[1]
    key_scaled = key_rows * scale
    values = qkv_ref[2]
    grad = grad_ref[...]
    first = lane_halves(key_rows.shape[0])
    grad_queries, grad_keys, grad_values = [], [], []
    for head in range(2):
        own = first if head == 0 else ~first
        zero = jnp.zeros_like(key_rows)
        scores = dot(jnp.where(own, key_rows, zero), queries, 1, 1) + mask_ref[...]
        probs = jnp.exp(scores - total_ref[0, 0, head : head + 1, :])
        grad_probs = dot(jnp.where(own, values, zero), grad, 1, 1)
        weighted = jnp.sum(probs * grad_probs, axis=0, keepdims=True)
        grad_scores = (probs * (grad_probs - weighted)).astype(BF16)
        grad_values.append(dot(probs.astype(BF16), grad, 1, 0))
        grad_keys.append(dot(grad_scores, queries, 1, 0))
        grad_queries.append(dot(key_scaled, grad_scores, 0, 0))
    joined = jnp.concatenate([grad_queries[0][:HD], grad_queries[1][HD:]], axis=0)
    out_ref[0] = joined.T.astype(BF16)
    out_ref[1] = jnp.where(first, grad_keys[0], grad_keys[1]).astype(BF16)
    out_ref[2] = jnp.where(first, grad_values[0], grad_values[1]).astype(BF16)


def attention_specs(seq_len):
    return dict(
        row=pl.BlockSpec((1, 1, seq_len), lambda r, h: (r, 0, 0)),
        col=pl.BlockSpec((1, seq_len, 1), lambda r, h: (r, 0, 0)),
        three=pl.BlockSpec((3, seq_len, 2 * HD), lambda r, h: (0, r, h)),
        one=pl.BlockSpec((seq_len, 2 * HD), lambda r, h: (r, h)),
        total=pl.BlockSpec((1, 1, 8, seq_len), lambda r, h: (r, h, 0, 0)),
    )


def attend(segments, qkv):
    rows, seq_len = segments.shape
    pairs = qkv.shape[2] // (2 * HD)
    s = attention_specs(seq_len)
    area = rows * pairs * 2 * seq_len * seq_len
    return pl.pallas_call(
        attend_kernel,
        grid=(rows, pairs),
        in_specs=[s["row"], s["col"], s["three"]],
        out_specs=[s["one"], s["total"]],
        out_shape=[
            jax.ShapeDtypeStruct(qkv.shape[1:], BF16),
            jax.ShapeDtypeStruct((rows, pairs, 8, seq_len), F32),
        ],
        scratch_shapes=[pltpu.VMEM((seq_len, seq_len), F32)],
        cost_estimate=pl.CostEstimate(
            flops=area * 512, bytes_accessed=qkv.size * 3, transcendentals=area
        ),
        name="attend",
    )(segments[:, None, :], segments[:, :, None], qkv)


def attend_back(segments, qkv, totals, grad):
    rows, seq_len = segments.shape
    pairs = qkv.shape[2] // (2 * HD)
    s = attention_specs(seq_len)
    area = rows * pairs * 2 * seq_len * seq_len
    return pl.pallas_call(
        attend_back_kernel,
        grid=(rows, pairs),
        in_specs=[s["row"], s["col"], s["three"], s["total"], s["one"]],
        out_specs=s["three"],
        out_shape=jax.ShapeDtypeStruct(qkv.shape, BF16),
        scratch_shapes=[pltpu.VMEM((seq_len, seq_len), F32)],
        cost_estimate=pl.CostEstimate(
            flops=area * 1280, bytes_accessed=qkv.size * 5, transcendentals=area
        ),
        name="attend_back",
    )(segments[:, None, :], segments[:, :, None], qkv, totals, grad)


def gelu_parts(value):
    size = jnp.abs(value)
    bell = jnp.exp(-0.5 * value * value)
    t = 1.0 / (1.0 + (0.3275911 / math.sqrt(2.0)) * size)
    series = 1.061405429 / 2
    for factor in (-1.453152027 / 2, 1.421413741 / 2, -0.284496736 / 2, 0.254829592 / 2):
        series = series * t + factor
    tail = series * t * bell
    cumulative = jnp.where(value < 0, tail, 1.0 - tail)
    return cumulative, value * bell * (1.0 / math.sqrt(2.0 * math.pi))


def forward_kernel(hidden_ref, in_ref, back_ref, bias_ref, act_ref, slope_ref, branch_ref):
    width = hidden_ref.shape[1]
    w_in = in_ref[...].reshape(-1, width)
    w_back = back_ref[...].reshape(width, -1)
    first = pl.program_id(0) == 0

    def body(tile, carry):
        rows = pl.ds(pl.multiple_of(tile * TILE, TILE), TILE)
        pre_act = dot(hidden_ref[rows, :], w_in, 1, 1) + bias_ref[...]
        cumulative, along = gelu_parts(pre_act)
        activation = (pre_act * cumulative).astype(BF16)
        act_ref[rows, :] = activation
        slope_ref[rows, :] = cumulative + along
        branch = dot(activation, w_back, 1, 1)
        branch_ref[rows, :] = branch + jnp.where(first, 0.0, branch_ref[rows, :])
        return carry

    lax.fori_loop(0, hidden_ref.shape[0] // TILE, body, 0)


def weight_specs(gathered, in_part, out_part):
    devices, rows, width = gathered.shape
    chunks = in_part * devices // width
    return (
        pl.BlockSpec((devices // chunks, in_part, width), lambda c: (c, 0, 0)),
        pl.BlockSpec((devices, out_part, width), lambda c: (0, in_part // out_part + c, 0)),
    )


def feed_forward(hidden, gathered, bias, in_part, out_part):
    tokens, width = hidden.shape
    units = bias.shape[0]
    whole = pl.BlockSpec((tokens, width), lambda c: (0, 0))
    chunk = pl.BlockSpec((tokens, width), lambda c: (0, c))
    return pl.pallas_call(
        forward_kernel,
        grid=(units // width,),
        in_specs=[
            whole,
            *weight_specs(gathered, in_part, out_part),
            pl.BlockSpec((1, width), lambda c: (0, c)),
        ],
        out_specs=[chunk, chunk, whole],
        out_shape=[
            jax.ShapeDtypeStruct((tokens, units), BF16),
            jax.ShapeDtypeStruct((tokens, units), F32),
            jax.ShapeDtypeStruct((tokens, width), F32),
        ],
        cost_estimate=pl.CostEstimate(
            flops=4 * tokens * width * units,
            bytes_accessed=6 * tokens * units,
            transcendentals=2 * tokens * units,
        ),
        name="feed_forward",
    )(hidden, gathered, gathered, bias[None])


def backward_kernel(
    grad_ref,
    hidden_ref,
    act_ref,
    slope_ref,
    in_ref,
    back_ref,
    grad_hidden_ref,
    bias_ref,
    terms_ref,
    turned,
    grad_pre,
    in_tile,
    back_tile,
    sems,
):
    step, steps = pl.program_id(0), pl.num_programs(0)
    slot = step % 2
    tokens, width = hidden_ref.shape
    _, shards, in_part, _ = in_tile.shape
    devices, out_part = back_tile.shape[1:3]
    w_in = in_ref[...].reshape(-1, width)
    w_back = back_ref[...].reshape(width, -1)

    def copies(at, place):
        return (
            pltpu.make_async_copy(
                in_tile.at[place],
                terms_ref.at[pl.ds(at * shards, shards), pl.ds(0, in_part)],
                sems.at[0, place],
            ),
            pltpu.make_async_copy(
                back_tile.at[place],
                terms_ref.at[:, pl.ds(pl.multiple_of(in_part + at * out_part, 8), out_part)],
                sems.at[1, place],
            ),
        )

    @pl.when(step == 0)
    def _():
        turned[...] = grad_ref[...].T

    @pl.when(step >= 2)
    def _():
        for copy in copies(step - 2, slot):
            copy.wait()

    def body(tile, total):
        rows = pl.ds(pl.multiple_of(tile * TILE, TILE), TILE)
        grad = (slope_ref[rows, :] * dot(grad_ref[rows, :], w_back, 1, 0)).astype(BF16)
        grad_pre[rows, :] = grad
        term = dot(grad, w_in, 1, 0)
        grad_hidden_ref[rows, :] = term + jnp.where(step == 0, 0.0, grad_hidden_ref[rows, :])
        return total + jnp.sum(grad.astype(F32), axis=0, keepdims=True)

    bias_ref[...] = lax.fori_loop(0, tokens // TILE, body, jnp.zeros((1, width), F32))
    half = width // 2

    def weights(part, carry):
        span = pl.ds(pl.multiple_of(part * half, half), half)
        term = dot(grad_pre[:, span], hidden_ref[...], 0, 0)
        in_tile[slot, pl.ds(part * (shards // 2), shards // 2)] = term.reshape(
            shards // 2, in_part, width
        ).astype(BF16)
        term = dot(turned[span, :], act_ref[...], 1, 0)
        back_tile[slot, pl.ds(part * (devices // 2), devices // 2)] = term.reshape(
            devices // 2, out_part, width
        ).astype(BF16)
        return carry

    lax.fori_loop(0, 2, weights, 0)
    for copy in copies(step, slot):
        copy.start()

    @pl.when(step == steps - 1)
    def _():
        for copy in copies(step - 1, 1 - slot) + copies(step, slot):
            copy.wait()


def feed_backward(grad, hidden, activation, slope, gathered, in_part, out_part):
    tokens, width = hidden.shape
    units = activation.shape[1]
    devices = gathered.shape[0]
    shards = width // in_part
    whole = pl.BlockSpec((tokens, width), lambda c: (0, 0))
    chunk = pl.BlockSpec((tokens, width), lambda c: (0, c))
    return pl.pallas_call(
        backward_kernel,
        grid=(units // width,),
        in_specs=[whole, whole, chunk, chunk, *weight_specs(gathered, in_part, out_part)],
        out_specs=[
            whole,
            pl.BlockSpec((1, width), lambda c: (0, c)),
            pl.BlockSpec(memory_space=pl.ANY),
        ],
        out_shape=[
            jax.ShapeDtypeStruct((tokens, width), F32),
            jax.ShapeDtypeStruct((1, units), F32),
            jax.ShapeDtypeStruct(gathered.shape, BF16),
        ],
        scratch_shapes=[
            pltpu.VMEM((width, tokens), BF16),
            pltpu.VMEM((tokens, width), BF16),
            pltpu.VMEM((2, shards, in_part, width), BF16),
            pltpu.VMEM((2, devices, out_part, width), BF16),
            pltpu.SemaphoreType.DMA((2, 2)),
        ],
        cost_estimate=pl.CostEstimate(
            flops=8 * tokens * width * units, bytes_accessed=10 * tokens * units, transcendentals=0
        ),
        name="feed_backward",
    )(grad, hidden, activation, slope, gathered, gathered)


def norm_stats(residual):
    average = jnp.mean(residual, axis=-1, keepdims=True)
    centred = residual - average
    spread = jnp.mean(centred * centred, axis=-1, keepdims=True)
    inverse = lax.rsqrt(spread + NORM_EPS)
    return centred * inverse, inverse


def norm_back(normal, inverse, grad, gain):
    weighted = grad * gain
    along = jnp.mean(weighted * normal, axis=-1, keepdims=True)
    return inverse * (weighted - jnp.mean(weighted, axis=-1, keepdims=True) - normal * along)


def sum_kernel(sizes, x_ref, out_ref, held, arrived, send_sem, recv_sem):
    partners = []
    for axis, size in sizes:
        index = lax.axis_index(axis)
        bit = 1
        while bit < size:
            partners.append({axis: index + bit - 2 * bit * ((index // bit) % 2)})
            bit *= 2
    barrier = pltpu.get_barrier_semaphore()
    for partner in partners:
        pl.semaphore_signal(barrier, 1, device_id=partner, device_id_type=MESH)
    pl.semaphore_wait(barrier, len(partners))
    held[0] = x_ref[...]
    for step, partner in enumerate(partners):
        copy = pltpu.make_async_remote_copy(
            src_ref=held.at[step],
            dst_ref=arrived.at[step],
            send_sem=send_sem.at[step],
            recv_sem=recv_sem.at[step],
            device_id=partner,
            device_id_type=MESH,
        )
        copy.start()
        copy.wait()
        held[step + 1] = held[step] + arrived[step]
    out_ref[...] = held[len(partners)]


def exchange_orders(dp_size):
    bits = list(range(dp_size.bit_length() - 2, -1, -1))
    return bits[:-1] + ["head", bits[-1]], bits[:-2] + ["head", bits[-2], bits[-1]]


def own_bit(bit):
    return lax.axis_index("head") if bit == "head" else (lax.axis_index("dp") // 2**bit) % 2


def partner_of(bit):
    index = lax.axis_index("head" if bit == "head" else "dp")
    step = 1 if bit == "head" else 2**bit
    return {"head" if bit == "head" else "dp": index + step - 2 * step * own_bit(bit)}


def meet(bits):
    barrier = pltpu.get_barrier_semaphore()
    for bit in bits:
        pl.semaphore_signal(barrier, 1, device_id=partner_of(bit), device_id_type=MESH)
    pl.semaphore_wait(barrier, len(bits))


def lanes_of(half, width):
    return pl.ds(pl.multiple_of(half * width, width), width)


def gather_kernel(dp_size, qkv_ref, out_ref, qkv_full, out_full, own_sem, send_sem, recv_sem):
    orders = exchange_orders(dp_size)
    bits = [bit for bit in orders[0] if bit != "head"]
    width = qkv_ref.shape[2]
    meet(orders[0])

    def qkv_view(kinds, done):
        index = tuple(slice(None) if bit in done else own_bit(bit) for bit in bits)
        lanes = slice(None) if "head" in done else lanes_of(own_bit("head"), width)
        return qkv_full.at[(kinds,) + index + (slice(None), lanes)]

    def out_view(done):
        return out_full.at[
            tuple(slice(None) if bit in done else own_bit(bit) for bit in bits + ["head"])
        ]

    own = [
        pltpu.make_async_copy(qkv_ref, qkv_view(slice(None), ()), own_sem.at[0]),
        pltpu.make_async_copy(out_ref, out_view(()), own_sem.at[1]),
    ]
    for copy in own:
        copy.start()
    for copy in own:
        copy.wait()
    for step in range(len(orders[0])):
        copies = []
        for stream in range(3):
            order = orders[0] if stream == 0 else orders[1]
            done = order[:step]
            if stream == 2:
                view = out_view(done)
            else:
                view = qkv_view(slice(0, 2) if stream == 0 else slice(2, 3), done)
            copies.append(
                pltpu.make_async_remote_copy(
                    src_ref=view,
                    dst_ref=view,
                    send_sem=send_sem.at[step, stream],
                    recv_sem=recv_sem.at[step, stream],
                    device_id=partner_of(order[step]),
                    device_id_type=MESH,
                )
            )
        for copy in copies:
            copy.start()
        for copy in copies:
            copy.wait()


def gather_projections(qkv_shard, out_shard, dp_size):
    _, part, own_width = qkv_shard.shape
    bits = (2,) * (dp_size.bit_length() - 1)
    steps = len(bits) + 1
    vmem = pl.BlockSpec(memory_space=pltpu.VMEM)
    qkv_full, out_full = pl.pallas_call(
        functools.partial(gather_kernel, dp_size),
        out_shape=[
            jax.ShapeDtypeStruct((3,) + bits + (part, 2 * own_width), BF16),
            jax.ShapeDtypeStruct(bits + (2,) + out_shard.shape, BF16),
        ],
        in_specs=[vmem, vmem],
        out_specs=[vmem, vmem],
        scratch_shapes=[
            pltpu.SemaphoreType.DMA((2,)),
            pltpu.SemaphoreType.DMA((steps, 3)),
            pltpu.SemaphoreType.DMA((steps, 3)),
        ],
        compiler_params=pltpu.CompilerParams(collective_id=1, has_side_effects=True),
        cost_estimate=pl.CostEstimate(flops=0, bytes_accessed=2**27, transcendentals=0),
        name="gather_projections",
    )(qkv_shard, out_shard)
    return (
        qkv_full.reshape(3, dp_size * part, 2 * own_width),
        out_full.reshape(dp_size * 2 * out_shard.shape[0], out_shard.shape[1]),
    )


def reduce_kernel(dp_size, qkv_ref, out_ref, qkv_sum, out_sum, *scratch):
    steps = len(exchange_orders(dp_size)[0])
    arrived, held = scratch[: 3 * steps], scratch[3 * steps : -2]
    send_sem, recv_sem = scratch[-2:]
    orders = [list(reversed(order)) for order in exchange_orders(dp_size)]
    meet(orders[0])
    bits = [bit for bit in orders[0] if bit != "head"]
    bits.sort(reverse=True)
    width = qkv_sum.shape[2]

    def view(ref, kinds, done, bit, half):
        index = tuple(half if b == bit else slice(None) for b in bits if b not in done)
        if kinds is None:
            if "head" not in done:
                index += (half if bit == "head" else slice(None),)
            return index
        lanes = lanes_of(half, width) if bit == "head" else slice(None)
        return (kinds,) + index + (slice(None), lanes)

    for step in range(steps):
        copies, mine = [], []
        for stream in range(3):
            order = orders[0] if stream == 0 else orders[1]
            bit, done = order[step], order[:step]
            if step == 0:
                source = out_ref if stream == 2 else qkv_ref
                kinds = (slice(0, 2), slice(2, 3), None)[stream]
            else:
                source = held[3 * (step - 1) + stream]
                kinds = None if stream == 2 else slice(None)
            target = arrived[3 * step + stream]
            copies.append(
                pltpu.make_async_remote_copy(
                    src_ref=source.at[view(source, kinds, done, bit, 1 - own_bit(bit))],
                    dst_ref=target,
                    send_sem=send_sem.at[step, stream],
                    recv_sem=recv_sem.at[step, stream],
                    device_id=partner_of(bit),
                    device_id_type=MESH,
                )
            )
            mine.append((source, view(source, kinds, done, bit, own_bit(bit)), target))
        for copy in copies:
            copy.start()
        for stream in range(3):
            copies[stream].wait()
            source, index, target = mine[stream]
            total = source[index].astype(F32) + target[...].astype(F32)
            if step < steps - 1:
                held[3 * step + stream][...] = total.astype(BF16)
            elif stream == 2:
                out_sum[...] = total
            elif stream == 0:
                qkv_sum[0:2] = total
            else:
                qkv_sum[2:3] = total


def reduce_projections(qkv_term, out_term, dp_size):
    count = dp_size.bit_length() - 1
    part, own_width = qkv_term.shape[1] // dp_size, qkv_term.shape[2] // 2
    out_part = out_term.shape[0] // (2 * dp_size)
    orders = [list(reversed(order)) for order in exchange_orders(dp_size)]
    shapes = []
    for step in range(count + 1):
        for stream in range(3):
            done = orders[0 if stream == 0 else 1][: step + 1]
            left = (2,) * (count - sum(bit != "head" for bit in done))
            if stream == 2:
                head = () if "head" in done else (2,)
                shapes.append(left + head + (out_part, out_term.shape[1]))
            else:
                wide = own_width if "head" in done else 2 * own_width
                shapes.append(((2, 1)[stream],) + left + (part, wide))
    vmem = pl.BlockSpec(memory_space=pltpu.VMEM)
    buffers = [pltpu.VMEM(shape, BF16) for shape in shapes]
    return pl.pallas_call(
        functools.partial(reduce_kernel, dp_size),
        out_shape=[
            jax.ShapeDtypeStruct((3, part, own_width), F32),
            jax.ShapeDtypeStruct((out_part, out_term.shape[1]), F32),
        ],
        in_specs=[vmem, vmem],
        out_specs=[vmem, vmem],
        scratch_shapes=buffers
        + buffers[: 3 * count]
        + [pltpu.SemaphoreType.DMA((count + 1, 3)), pltpu.SemaphoreType.DMA((count + 1, 3))],
        compiler_params=pltpu.CompilerParams(collective_id=2, has_side_effects=True),
        cost_estimate=pl.CostEstimate(flops=0, bytes_accessed=2**27, transcendentals=0),
        name="reduce_projections",
    )(
        qkv_term.reshape((3,) + (2,) * count + (part, 2 * own_width)),
        out_term.reshape((2,) * (count + 1) + (out_part, out_term.shape[1])),
    )


def sum_everywhere(x, sizes):
    steps = sum(size.bit_length() - 1 for _, size in sizes)
    return pl.pallas_call(
        functools.partial(sum_kernel, sizes),
        out_shape=jax.ShapeDtypeStruct(x.shape, x.dtype),
        in_specs=[pl.BlockSpec(memory_space=pltpu.VMEM)],
        out_specs=pl.BlockSpec(memory_space=pltpu.VMEM),
        scratch_shapes=[
            pltpu.VMEM((steps + 1,) + x.shape, x.dtype),
            pltpu.VMEM((steps,) + x.shape, x.dtype),
            pltpu.SemaphoreType.DMA((steps,)),
            pltpu.SemaphoreType.DMA((steps,)),
        ],
        compiler_params=pltpu.CompilerParams(collective_id=0, has_side_effects=True),
        name="sum_everywhere",
    )(x)


def on_device(
    tokens,
    segment_ids,
    w_qkv,
    qv_bias,
    w_out,
    out_bias,
    w_in,
    in_bias,
    w_back,
    back_bias,
    norm_gains,
    norm_shifts,
    out_cotangent,
    *,
    dp_size,
    head_size,
):
    micro, local, width = tokens.shape
    seq_len = segment_ids.shape[2]
    own_rows = local // seq_len

    devices = dp_size * head_size
    hidden_width = in_bias.shape[0]
    out_part, in_part = width // devices, hidden_width // devices
    chunks = hidden_width // width
    back_part = chunks * out_part
    packed = jnp.concatenate(
        [
            w_in.T,
            w_back.reshape(chunks, width, out_part).transpose(0, 2, 1).reshape(back_part, width),
        ]
    )
    gathered = lax.all_gather(packed, AXES, axis=0, tiled=False)
    fits = in_part % 16 == 0 and out_part % 8 == 0 and micro * local % TILE == 0
    qkv_full, out_full = gather_projections(w_qkv, w_out.T, dp_size)

    x = tokens.reshape(micro * local, width)
    segments = lax.dynamic_slice_in_dim(
        segment_ids, lax.axis_index("head") * own_rows, own_rows, 1
    ).reshape(micro * own_rows, seq_len)
    bias = jnp.stack([qv_bias[0], jnp.zeros_like(qv_bias[0]), qv_bias[1]])[:, None, :]
    qkv = (
        jnp.einsum("td,cdf->ctf", x, qkv_full, preferred_element_type=F32) + bias
    ).astype(BF16)
    context, totals = attend(segments, qkv)
    attended = dot(context, out_full, 1, 1) + out_bias
    normal_one, inverse_one = norm_stats(x.astype(F32) + attended)
    hidden = normal_one * norm_gains[0] + norm_shifts[0]
    hidden_low = hidden.astype(BF16)
    if fits:
        activation, slope, branch = feed_forward(
            hidden_low, gathered, in_bias, in_part, out_part
        )
    else:
        in_full = gathered[:, :in_part].reshape(hidden_width, width)
        back_full = (
            gathered[:, in_part:]
            .reshape(devices, chunks, out_part, width)
            .transpose(0, 2, 1, 3)
            .reshape(width, hidden_width)
        )
        pre_act = dot(hidden_low, in_full, 1, 1) + in_bias
        cumulative, along = gelu_parts(pre_act)
        activation = (pre_act * cumulative).astype(BF16)
        slope = cumulative + along
        branch = dot(activation, back_full, 1, 1)
    branch = branch + back_bias
    normal_two, inverse_two = norm_stats(hidden + branch)
    out = (normal_two * norm_gains[1] + norm_shifts[1]).astype(BF16)

    error = out_cotangent.reshape(micro * local, width).astype(F32)
    grad_two = norm_back(normal_two, inverse_two, error, norm_gains[1])
    gain_two = jnp.sum(error * normal_two, axis=0)
    shift_two = jnp.sum(error, axis=0)
    grad_branch = grad_two.astype(BF16)
    if fits:
        grad_hidden, in_bias_sum, terms = feed_backward(
            grad_branch, hidden_low, activation, slope, gathered, in_part, out_part
        )
    else:
        back_term = dot(grad_branch, activation, 0, 0).astype(BF16)
        grad_pre = (slope * dot(grad_branch, back_full, 1, 0)).astype(BF16)
        in_term = dot(grad_pre, hidden_low, 0, 0).astype(BF16)
        back_term = (
            back_term.reshape(devices, out_part, chunks, width)
            .transpose(0, 2, 1, 3)
            .reshape(devices, back_part, width)
        )
        terms = jnp.concatenate(
            [
                in_term.reshape(devices, in_part, width),
                back_term,
            ],
            axis=1,
        )
        grad_hidden = dot(grad_pre, in_full, 1, 0)
        in_bias_sum = jnp.sum(grad_pre.astype(F32), axis=0)
    summed = lax.psum_scatter(terms, AXES, scatter_dimension=0, tiled=False).astype(F32)
    grad_hidden = grad_two + grad_hidden
    grad_one = norm_back(normal_one, inverse_one, grad_hidden, norm_gains[0])
    gain_one = jnp.sum(grad_hidden * normal_one, axis=0)
    shift_one = jnp.sum(grad_hidden, axis=0)
    grad_attn = grad_one.astype(BF16)
    out_term = dot(grad_attn, context, 0, 0).astype(BF16)
    grad_context = dot(grad_attn, out_full, 1, 0).astype(BF16)
    grad_qkv = attend_back(segments, qkv, totals, grad_context)
    term = jnp.einsum("td,ctf->cdf", x, grad_qkv, preferred_element_type=F32)
    qkv_grad, out_grad = reduce_projections(term.astype(BF16), out_term, dp_size)
    x_grad = grad_one + jnp.einsum(
        "ctf,cdf->td", grad_qkv, qkv_full, preferred_element_type=F32
    )
    small = jnp.concatenate(
        [
            jnp.sum(grad_qkv[0].astype(F32), axis=0),
            jnp.sum(grad_qkv[2].astype(F32), axis=0),
            jnp.sum(grad_attn.astype(F32), axis=0),
            in_bias_sum.reshape(-1),
            jnp.sum(grad_branch.astype(F32), axis=0),
            gain_one,
            gain_two,
            shift_one,
            shift_two,
        ]
    )
    small = sum_everywhere(
        small.reshape(-1, 128), (("dp", dp_size), ("head", head_size))
    ).reshape(-1)
    cuts, at = [], 0
    for size in (2 * width, width, hidden_width, width, 2 * width, 2 * width):
        cuts.append(small[at : at + size])
        at += size
    return (
        out.reshape(tokens.shape),
        x_grad.reshape(tokens.shape),
        qkv_grad,
        cuts[0].reshape(2, width),
        out_grad.T,
        cuts[1],
        summed[:in_part].T,
        cuts[2],
        summed[in_part:]
        .reshape(chunks, out_part, width)
        .transpose(0, 2, 1)
        .reshape(hidden_width, out_part),
        cuts[3],
        cuts[4].reshape(2, width),
        cuts[5].reshape(2, width),
    )


def solution(mesh):
    return jax.shard_map(
        functools.partial(
            on_device, dp_size=mesh.shape["dp"], head_size=mesh.shape["head"]
        ),
        mesh=mesh,
        in_specs=(
            P(None, AXES, None),
            P(None, "dp", None),
            P(None, "dp", "head"),
            P(),
            P(None, AXES),
            P(),
            P(None, AXES),
            P(),
            P(None, AXES),
            P(),
            P(),
            P(),
            P(None, AXES, None),
        ),
        out_specs=(
            P(None, AXES, None),
            P(None, AXES, None),
            P(None, "dp", "head"),
            P(),
            P(None, AXES),
            P(),
            P(None, AXES),
            P(),
            P(None, AXES),
            P(),
            P(),
            P(),
        ),
        check_vma=False,
    )
```

```python
import functools
import math

import jax
import jax.numpy as jnp
from jax import lax
from jax.experimental import pallas as pl
from jax.experimental.pallas import tpu as pltpu
from jax.sharding import PartitionSpec as P

HD = 64
NORM_EPS = 1e-05
MASKED = -1e30
AXES = ("dp", "head")
F32 = jnp.float32
BF16 = jnp.bfloat16
MESH = pl.DeviceIdType.MESH
TILE = 256


def dot(left, right, left_dim, right_dim):
    return lax.dot_general(
        left, right, (((left_dim,), (right_dim,)), ((), ())), preferred_element_type=F32
    )


def fill_mask(segment_row, segment_col, mask_ref):
    @pl.when(pl.program_id(1) == 0)
    def _():
        mask_ref[...] = jnp.where(segment_col[0] == segment_row[0], 0.0, MASKED)


def lane_halves(rows):
    lane = lax.broadcasted_iota(jnp.int32, (rows, 2 * HD), 1)
    return lane < HD


def attend_kernel(seg_row, seg_col, qkv_ref, context_ref, total_ref, mask_ref):
    fill_mask(seg_row, seg_col, mask_ref)
    queries = qkv_ref[0] * jnp.asarray(HD**-0.5, BF16)
    key_rows = qkv_ref[1]
    values = qkv_ref[2]
    first = lane_halves(key_rows.shape[0])
    parts = []
    for head in range(2):
        keys_own = jnp.where(first if head == 0 else ~first, key_rows, jnp.zeros_like(key_rows))
        scores = dot(keys_own, queries, 1, 1) + mask_ref[...]
        highest = jnp.max(scores, axis=0, keepdims=True)
        exponent = jnp.exp(scores - highest)
        totals = jnp.sum(exponent, axis=0, keepdims=True)
        low = (exponent * (1.0 / totals)).astype(BF16)
        total_ref[0, 0, head : head + 1, :] = highest + jnp.log(totals)
        parts.append(dot(values, low, 0, 0))
    joined = jnp.concatenate([parts[0][:HD], parts[1][HD:]], axis=0)
    context_ref[...] = joined.T.astype(BF16)


def attend_back_kernel(seg_row, seg_col, qkv_ref, total_ref, grad_ref, out_ref, mask_ref):
    fill_mask(seg_row, seg_col, mask_ref)
    scale = jnp.asarray(HD**-0.5, BF16)
    queries = qkv_ref[0] * scale
    key_rows = qkv_ref[1]
    key_scaled = key_rows * scale
    values = qkv_ref[2]
    grad = grad_ref[...]
    first = lane_halves(key_rows.shape[0])
    grad_queries, grad_keys, grad_values = [], [], []
    for head in range(2):
        own = first if head == 0 else ~first
        zero = jnp.zeros_like(key_rows)
        scores = dot(jnp.where(own, key_rows, zero), queries, 1, 1) + mask_ref[...]
        probs = jnp.exp(scores - total_ref[0, 0, head : head + 1, :])
        grad_probs = dot(jnp.where(own, values, zero), grad, 1, 1)
        weighted = jnp.sum(probs * grad_probs, axis=0, keepdims=True)
        grad_scores = (probs * (grad_probs - weighted)).astype(BF16)
        grad_values.append(dot(probs.astype(BF16), grad, 1, 0))
        grad_keys.append(dot(grad_scores, queries, 1, 0))
        grad_queries.append(dot(key_scaled, grad_scores, 0, 0))
    joined = jnp.concatenate([grad_queries[0][:HD], grad_queries[1][HD:]], axis=0)
    out_ref[0] = joined.T.astype(BF16)
    out_ref[1] = jnp.where(first, grad_keys[0], grad_keys[1]).astype(BF16)
    out_ref[2] = jnp.where(first, grad_values[0], grad_values[1]).astype(BF16)


def attention_specs(seq_len):
    return dict(
        row=pl.BlockSpec((1, 1, seq_len), lambda r, h: (r, 0, 0)),
        col=pl.BlockSpec((1, seq_len, 1), lambda r, h: (r, 0, 0)),
        three=pl.BlockSpec((3, seq_len, 2 * HD), lambda r, h: (0, r, h)),
        one=pl.BlockSpec((seq_len, 2 * HD), lambda r, h: (r, h)),
        total=pl.BlockSpec((1, 1, 8, seq_len), lambda r, h: (r, h, 0, 0)),
    )


def attend(segments, qkv):
    rows, seq_len = segments.shape
    pairs = qkv.shape[2] // (2 * HD)
    s = attention_specs(seq_len)
    area = rows * pairs * 2 * seq_len * seq_len
    return pl.pallas_call(
        attend_kernel,
        grid=(rows, pairs),
        in_specs=[s["row"], s["col"], s["three"]],
        out_specs=[s["one"], s["total"]],
        out_shape=[
            jax.ShapeDtypeStruct(qkv.shape[1:], BF16),
            jax.ShapeDtypeStruct((rows, pairs, 8, seq_len), F32),
        ],
        scratch_shapes=[pltpu.VMEM((seq_len, seq_len), F32)],
        cost_estimate=pl.CostEstimate(
            flops=area * 512, bytes_accessed=qkv.size * 3, transcendentals=area
        ),
        name="attend",
    )(segments[:, None, :], segments[:, :, None], qkv)


def attend_back(segments, qkv, totals, grad):
    rows, seq_len = segments.shape
    pairs = qkv.shape[2] // (2 * HD)
    s = attention_specs(seq_len)
    area = rows * pairs * 2 * seq_len * seq_len
    return pl.pallas_call(
        attend_back_kernel,
        grid=(rows, pairs),
        in_specs=[s["row"], s["col"], s["three"], s["total"], s["one"]],
        out_specs=s["three"],
        out_shape=jax.ShapeDtypeStruct(qkv.shape, BF16),
        scratch_shapes=[pltpu.VMEM((seq_len, seq_len), F32)],
        cost_estimate=pl.CostEstimate(
            flops=area * 1280, bytes_accessed=qkv.size * 5, transcendentals=area
        ),
        name="attend_back",
    )(segments[:, None, :], segments[:, :, None], qkv, totals, grad)


def gelu_parts(value, reciprocal=lambda v: 1.0 / v):
    size = jnp.abs(value)
    bell = jnp.exp2(value * value * (-0.5 / math.log(2.0)))
    t = reciprocal(1.0 + (0.3275911 / math.sqrt(2.0)) * size)
    series = 1.061405429 / 2
    for factor in (-1.453152027 / 2, 1.421413741 / 2, -0.284496736 / 2, 0.254829592 / 2):
        series = series * t + factor
    tail = series * t * bell
    cumulative = jnp.where(value < 0, tail, 1.0 - tail)
    return cumulative, value * bell * (1.0 / math.sqrt(2.0 * math.pi))


def forward_kernel(hidden_ref, in_ref, back_ref, bias_ref, act_ref, slope_ref, branch_ref):
    width = hidden_ref.shape[1]
    w_in = in_ref[...].reshape(-1, width)
    w_back = back_ref[...].reshape(width, -1)
    first = pl.program_id(0) == 0

    def body(tile, carry):
        rows = pl.ds(pl.multiple_of(tile * TILE, TILE), TILE)
        pre_act = dot(hidden_ref[rows, :], w_in, 1, 1) + bias_ref[...]
        cumulative, along = gelu_parts(pre_act, pl.reciprocal)
        activation = (pre_act * cumulative).astype(BF16)
        act_ref[rows, :] = activation
        slope_ref[rows, :] = cumulative + along
        branch = dot(activation, w_back, 1, 1)
        branch_ref[rows, :] = branch + jnp.where(first, 0.0, branch_ref[rows, :])
        return carry

    lax.fori_loop(0, hidden_ref.shape[0] // TILE, body, 0, unroll=2)


def weight_specs(gathered, in_part, out_part):
    devices, rows, width = gathered.shape
    chunks = in_part * devices // width
    return (
        pl.BlockSpec((devices // chunks, in_part, width), lambda c: (c, 0, 0)),
        pl.BlockSpec((devices, out_part, width), lambda c: (0, in_part // out_part + c, 0)),
    )


def feed_forward(hidden, gathered, bias, in_part, out_part):
    tokens, width = hidden.shape
    units = bias.shape[0]
    whole = pl.BlockSpec((tokens, width), lambda c: (0, 0))
    chunk = pl.BlockSpec((tokens, width), lambda c: (0, c))
    return pl.pallas_call(
        forward_kernel,
        grid=(units // width,),
        in_specs=[
            whole,
            *weight_specs(gathered, in_part, out_part),
            pl.BlockSpec((1, width), lambda c: (0, c)),
        ],
        out_specs=[chunk, chunk, whole],
        out_shape=[
            jax.ShapeDtypeStruct((tokens, units), BF16),
            jax.ShapeDtypeStruct((tokens, units), F32),
            jax.ShapeDtypeStruct((tokens, width), F32),
        ],
        cost_estimate=pl.CostEstimate(
            flops=4 * tokens * width * units,
            bytes_accessed=6 * tokens * units,
            transcendentals=2 * tokens * units,
        ),
        name="feed_forward",
    )(hidden, gathered, gathered, bias[None])


def backward_kernel(
    grad_ref,
    hidden_ref,
    act_ref,
    slope_ref,
    in_ref,
    back_ref,
    grad_hidden_ref,
    bias_ref,
    in_terms,
    back_terms,
    turned,
    grad_pre,
    in_tile,
    back_tile,
    sems,
):
    step, steps = pl.program_id(0), pl.num_programs(0)
    slot = step % 2
    tokens, width = hidden_ref.shape
    _, shards, in_part, _ = in_tile.shape
    devices, out_part = back_tile.shape[1:3]
    w_in = in_ref[...].reshape(-1, width)
    w_back = back_ref[...].reshape(width, -1)

    def copies(at, place):
        return (
            pltpu.make_async_copy(
                in_tile.at[place],
                in_terms.at[pl.ds(at * shards, shards)],
                sems.at[0, place],
            ),
            pltpu.make_async_copy(
                back_tile.at[place],
                back_terms.at[:, pl.ds(pl.multiple_of(at * out_part, 8), out_part)],
                sems.at[1, place],
            ),
        )

    @pl.when(step == 0)
    def _():
        turned[...] = grad_ref[...].T

    @pl.when(step >= 2)
    def _():
        for copy in copies(step - 2, slot):
            copy.wait()

    def body(tile, total):
        rows = pl.ds(pl.multiple_of(tile * TILE, TILE), TILE)
        grad = (slope_ref[rows, :] * dot(grad_ref[rows, :], w_back, 1, 0)).astype(BF16)
        grad_pre[rows, :] = grad
        term = dot(grad, w_in, 1, 0)
        grad_hidden_ref[rows, :] = term + jnp.where(step == 0, 0.0, grad_hidden_ref[rows, :])
        return total + jnp.sum(grad.astype(F32), axis=0, keepdims=True)

    bias_ref[...] = lax.fori_loop(0, tokens // TILE, body, jnp.zeros((1, width), F32))
    half = width // 2

    def weights(part, carry):
        span = pl.ds(pl.multiple_of(part * half, half), half)
        term = dot(grad_pre[:, span], hidden_ref[...], 0, 0)
        in_tile[slot, pl.ds(part * (shards // 2), shards // 2)] = term.reshape(
            shards // 2, in_part, width
        ).astype(BF16)
        term = dot(turned[span, :], act_ref[...], 1, 0)
        back_tile[slot, pl.ds(part * (devices // 2), devices // 2)] = term.reshape(
            devices // 2, out_part, width
        ).astype(BF16)
        return carry

    lax.fori_loop(0, 2, weights, 0)
    for copy in copies(step, slot):
        copy.start()

    @pl.when(step == steps - 1)
    def _():
        for copy in copies(step - 1, 1 - slot) + copies(step, slot):
            copy.wait()


class Halving:
    def __init__(self, terms, dp_size):
        count = dp_size.bit_length() - 1
        self.dp_size = dp_size
        self.orders = [list(reversed(order)) for order in exchange_orders(dp_size)]
        names = list(range(count - 1, -1, -1)) + ["head"]
        self.parts = [terms.reshape((2,) * (count + 1) + terms.shape[1:])]
        self.lefts = [names]
        self.at = 0

    def fold(self, held, left, bit):
        axis, size = ("head", 2) if bit == "head" else ("dp", self.dp_size)
        step = 1 if bit == "head" else 2**bit
        place, own = left.index(bit), own_bit(bit)
        give = lax.dynamic_index_in_dim(held, 1 - own, place, keepdims=False)
        keep = lax.dynamic_index_in_dim(held, own, place, keepdims=False)
        came = lax.ppermute(give, axis, [(i, i ^ step) for i in range(size)])
        return (keep, came), [b for b in left if b != bit]

    def step(self, values):
        if self.at == 1:
            half = self.parts[0].shape[-2] // 2
            self.parts = [self.parts[0][..., :half, :], self.parts[0][..., half:, :]]
            self.lefts = self.lefts * 2
        pairs = []
        for stream, part in enumerate(self.parts):
            pair, self.lefts[stream] = self.fold(
                part, self.lefts[stream], self.orders[stream][self.at]
            )
            pairs.append(pair)
        self.at += 1
        pairs, values = lax.optimization_barrier((pairs, values))
        self.parts = [
            (keep.astype(F32) + came.astype(F32)).astype(BF16) for keep, came in pairs
        ]
        return values

    def total(self):
        while self.at < len(self.orders[0]):
            self.step(())
        return jnp.concatenate(self.parts)


def feed_backward(grad, hidden, activation, slope, gathered, in_part, out_part):
    tokens, width = hidden.shape
    units = activation.shape[1]
    devices = gathered.shape[0]
    shards = width // in_part
    whole = pl.BlockSpec((tokens, width), lambda c: (0, 0))
    chunk = pl.BlockSpec((tokens, width), lambda c: (0, c))
    return pl.pallas_call(
        backward_kernel,
        grid=(units // width,),
        in_specs=[whole, whole, chunk, chunk, *weight_specs(gathered, in_part, out_part)],
        out_specs=[
            whole,
            pl.BlockSpec((1, width), lambda c: (0, c)),
            pl.BlockSpec(memory_space=pl.ANY),
            pl.BlockSpec(memory_space=pl.ANY),
        ],
        out_shape=[
            jax.ShapeDtypeStruct((tokens, width), F32),
            jax.ShapeDtypeStruct((1, units), F32),
            jax.ShapeDtypeStruct((devices, in_part, width), BF16),
            jax.ShapeDtypeStruct((devices, units // width * out_part, width), BF16),
        ],
        scratch_shapes=[
            pltpu.VMEM((width, tokens), BF16),
            pltpu.VMEM((tokens, width), BF16),
            pltpu.VMEM((2, shards, in_part, width), BF16),
            pltpu.VMEM((2, devices, out_part, width), BF16),
            pltpu.SemaphoreType.DMA((2, 2)),
        ],
        cost_estimate=pl.CostEstimate(
            flops=8 * tokens * width * units, bytes_accessed=10 * tokens * units, transcendentals=0
        ),
        name="feed_backward",
    )(grad, hidden, activation, slope, gathered, gathered)


def norm_stats(residual):
    average = jnp.mean(residual, axis=-1, keepdims=True)
    centred = residual - average
    spread = jnp.mean(centred * centred, axis=-1, keepdims=True)
    inverse = lax.rsqrt(spread + NORM_EPS)
    return centred * inverse, inverse


def norm_back(normal, inverse, grad, gain):
    weighted = grad * gain
    along = jnp.mean(weighted * normal, axis=-1, keepdims=True)
    return inverse * (weighted - jnp.mean(weighted, axis=-1, keepdims=True) - normal * along)


def exchange_orders(dp_size):
    bits = list(range(dp_size.bit_length() - 2, -1, -1))
    return bits[:-1] + ["head", bits[-1]], bits[:-2] + ["head", bits[-2], bits[-1]]


def own_bit(bit):
    return lax.axis_index("head") if bit == "head" else (lax.axis_index("dp") // 2**bit) % 2


def partner_of(bit):
    index = lax.axis_index("head" if bit == "head" else "dp")
    step = 1 if bit == "head" else 2**bit
    return {"head" if bit == "head" else "dp": index + step - 2 * step * own_bit(bit)}


def meet(bits):
    barrier = pltpu.get_barrier_semaphore()
    for bit in bits:
        pl.semaphore_signal(barrier, 1, device_id=partner_of(bit), device_id_type=MESH)
    pl.semaphore_wait(barrier, len(bits))


def lanes_of(half, width):
    return pl.ds(pl.multiple_of(half * width, width), width)


def gather_kernel(dp_size, qkv_ref, out_ref, qkv_full, out_full, own_sem, send_sem, recv_sem):
    orders = exchange_orders(dp_size)
    bits = [bit for bit in orders[0] if bit != "head"]
    width = qkv_ref.shape[2]
    meet(orders[0])

    def qkv_view(kinds, done):
        index = tuple(slice(None) if bit in done else own_bit(bit) for bit in bits)
        lanes = slice(None) if "head" in done else lanes_of(own_bit("head"), width)
        return qkv_full.at[(kinds,) + index + (slice(None), lanes)]

    def out_view(done):
        return out_full.at[
            tuple(slice(None) if bit in done else own_bit(bit) for bit in bits + ["head"])
        ]

    own = [
        pltpu.make_async_copy(qkv_ref, qkv_view(slice(None), ()), own_sem.at[0]),
        pltpu.make_async_copy(out_ref, out_view(()), own_sem.at[1]),
    ]
    for copy in own:
        copy.start()
    for copy in own:
        copy.wait()
    for step in range(len(orders[0])):
        copies = []
        for stream in range(3):
            order = orders[0] if stream == 0 else orders[1]
            done = order[:step]
            if stream == 2:
                view = out_view(done)
            else:
                view = qkv_view(slice(0, 2) if stream == 0 else slice(2, 3), done)
            copies.append(
                pltpu.make_async_remote_copy(
                    src_ref=view,
                    dst_ref=view,
                    send_sem=send_sem.at[step, stream],
                    recv_sem=recv_sem.at[step, stream],
                    device_id=partner_of(order[step]),
                    device_id_type=MESH,
                )
            )
        for copy in copies:
            copy.start()
        for copy in copies:
            copy.wait()


def gather_projections(qkv_shard, out_shard, dp_size):
    _, part, own_width = qkv_shard.shape
    bits = (2,) * (dp_size.bit_length() - 1)
    steps = len(bits) + 1
    vmem = pl.BlockSpec(memory_space=pltpu.VMEM)
    qkv_full, out_full = pl.pallas_call(
        functools.partial(gather_kernel, dp_size),
        out_shape=[
            jax.ShapeDtypeStruct((3,) + bits + (part, 2 * own_width), BF16),
            jax.ShapeDtypeStruct(bits + (2,) + out_shard.shape, BF16),
        ],
        in_specs=[vmem, vmem],
        out_specs=[vmem, vmem],
        scratch_shapes=[
            pltpu.SemaphoreType.DMA((2,)),
            pltpu.SemaphoreType.DMA((steps, 3)),
            pltpu.SemaphoreType.DMA((steps, 3)),
        ],
        compiler_params=pltpu.CompilerParams(collective_id=1, has_side_effects=True),
        cost_estimate=pl.CostEstimate(flops=0, bytes_accessed=2**27, transcendentals=0),
        name="gather_projections",
    )(qkv_shard, out_shard)
    return (
        qkv_full.reshape(3, dp_size * part, 2 * own_width),
        out_full.reshape(dp_size * 2 * out_shard.shape[0], out_shard.shape[1]),
    )


def reduce_kernel(
    dp_size, qkv_ref, out_ref, small_ref, qkv_sum, out_sum, small_sum, small_held, small_in, *scratch
):
    steps = len(exchange_orders(dp_size)[0])
    arrived, held = scratch[: 3 * steps], scratch[3 * steps : -2]
    send_sem, recv_sem = scratch[-2:]
    small_held[0] = small_ref[...]
    orders = [list(reversed(order)) for order in exchange_orders(dp_size)]
    meet(orders[0])
    bits = [bit for bit in orders[0] if bit != "head"]
    bits.sort(reverse=True)
    width = qkv_sum.shape[2]

    def view(ref, kinds, done, bit, half):
        index = tuple(half if b == bit else slice(None) for b in bits if b not in done)
        if kinds is None:
            if "head" not in done:
                index += (half if bit == "head" else slice(None),)
            return index
        lanes = lanes_of(half, width) if bit == "head" else slice(None)
        return (kinds,) + index + (slice(None), lanes)

    for step in range(steps):
        copies, mine = [], []
        for stream in range(3):
            order = orders[0] if stream == 0 else orders[1]
            bit, done = order[step], order[:step]
            if step == 0:
                source = out_ref if stream == 2 else qkv_ref
                kinds = (slice(0, 2), slice(2, 3), None)[stream]
            else:
                source = held[3 * (step - 1) + stream]
                kinds = None if stream == 2 else slice(None)
            target = arrived[3 * step + stream]
            copies.append(
                pltpu.make_async_remote_copy(
                    src_ref=source.at[view(source, kinds, done, bit, 1 - own_bit(bit))],
                    dst_ref=target,
                    send_sem=send_sem.at[step, stream],
                    recv_sem=recv_sem.at[step, stream],
                    device_id=partner_of(bit),
                    device_id_type=MESH,
                )
            )
            mine.append((source, view(source, kinds, done, bit, own_bit(bit)), target))
        copies.append(
            pltpu.make_async_remote_copy(
                src_ref=small_held.at[step],
                dst_ref=small_in.at[step],
                send_sem=send_sem.at[step, 3],
                recv_sem=recv_sem.at[step, 3],
                device_id=partner_of(orders[0][step]),
                device_id_type=MESH,
            )
        )
        for copy in copies:
            copy.start()
        for stream in range(3):
            copies[stream].wait()
            source, index, target = mine[stream]
            total = source[index].astype(F32) + target[...].astype(F32)
            if step < steps - 1:
                held[3 * step + stream][...] = total.astype(BF16)
            elif stream == 2:
                out_sum[...] = total
            elif stream == 0:
                qkv_sum[0:2] = total
            else:
                qkv_sum[2:3] = total
        copies[3].wait()
        small_held[step + 1] = small_held[step] + small_in[step]
    small_sum[...] = small_held[steps]


def reduce_projections(qkv_term, out_term, small, dp_size):
    count = dp_size.bit_length() - 1
    part, own_width = qkv_term.shape[1] // dp_size, qkv_term.shape[2] // 2
    out_part = out_term.shape[0] // (2 * dp_size)
    orders = [list(reversed(order)) for order in exchange_orders(dp_size)]
    shapes = []
    for step in range(count + 1):
        for stream in range(3):
            done = orders[0 if stream == 0 else 1][: step + 1]
            left = (2,) * (count - sum(bit != "head" for bit in done))
            if stream == 2:
                head = () if "head" in done else (2,)
                shapes.append(left + head + (out_part, out_term.shape[1]))
            else:
                wide = own_width if "head" in done else 2 * own_width
                shapes.append(((2, 1)[stream],) + left + (part, wide))
    vmem = pl.BlockSpec(memory_space=pltpu.VMEM)
    buffers = [pltpu.VMEM(shape, BF16) for shape in shapes]
    return pl.pallas_call(
        functools.partial(reduce_kernel, dp_size),
        out_shape=[
            jax.ShapeDtypeStruct((3, part, own_width), F32),
            jax.ShapeDtypeStruct((out_part, out_term.shape[1]), F32),
            jax.ShapeDtypeStruct(small.shape, F32),
        ],
        in_specs=[vmem, vmem, vmem],
        out_specs=[vmem, vmem, vmem],
        scratch_shapes=[
            pltpu.VMEM((count + 2,) + small.shape, F32),
            pltpu.VMEM((count + 1,) + small.shape, F32),
        ]
        + buffers
        + buffers[: 3 * count]
        + [pltpu.SemaphoreType.DMA((count + 1, 4)), pltpu.SemaphoreType.DMA((count + 1, 4))],
        compiler_params=pltpu.CompilerParams(collective_id=2, has_side_effects=True),
        cost_estimate=pl.CostEstimate(flops=0, bytes_accessed=2**27, transcendentals=0),
        name="reduce_projections",
    )(
        qkv_term.reshape((3,) + (2,) * count + (part, 2 * own_width)),
        out_term.reshape((2,) * (count + 1) + (out_part, out_term.shape[1])),
        small,
    )


def sum_everywhere(x, sizes):
    steps = sum(size.bit_length() - 1 for _, size in sizes)
    return pl.pallas_call(
        functools.partial(sum_kernel, sizes),
        out_shape=jax.ShapeDtypeStruct(x.shape, x.dtype),
        in_specs=[pl.BlockSpec(memory_space=pltpu.VMEM)],
        out_specs=pl.BlockSpec(memory_space=pltpu.VMEM),
        scratch_shapes=[
            pltpu.VMEM((steps + 1,) + x.shape, x.dtype),
            pltpu.VMEM((steps,) + x.shape, x.dtype),
            pltpu.SemaphoreType.DMA((steps,)),
            pltpu.SemaphoreType.DMA((steps,)),
        ],
        compiler_params=pltpu.CompilerParams(collective_id=0, has_side_effects=True),
        name="sum_everywhere",
    )(x)


def on_device(
    tokens,
    segment_ids,
    w_qkv,
    qv_bias,
    w_out,
    out_bias,
    w_in,
    in_bias,
    w_back,
    back_bias,
    norm_gains,
    norm_shifts,
    out_cotangent,
    *,
    dp_size,
    head_size,
):
    micro, local, width = tokens.shape
    seq_len = segment_ids.shape[2]
    own_rows = local // seq_len

    devices = dp_size * head_size
    hidden_width = in_bias.shape[0]
    out_part, in_part = width // devices, hidden_width // devices
    chunks = hidden_width // width
    back_part = chunks * out_part
    packed = jnp.concatenate(
        [
            w_in.T,
            w_back.reshape(chunks, width, out_part).transpose(0, 2, 1).reshape(back_part, width),
        ]
    )
    gathered = lax.all_gather(packed, AXES, axis=0, tiled=False)
    fits = in_part % 16 == 0 and out_part % 8 == 0 and micro * local % TILE == 0
    qkv_full, out_full = gather_projections(w_qkv, w_out.T, dp_size)

    x = tokens.reshape(micro * local, width)
    segments = lax.dynamic_slice_in_dim(
        segment_ids, lax.axis_index("head") * own_rows, own_rows, 1
    ).reshape(micro * own_rows, seq_len)
    bias = jnp.stack([qv_bias[0], jnp.zeros_like(qv_bias[0]), qv_bias[1]])[:, None, :]
    qkv = (
        jnp.einsum("td,cdf->ctf", x, qkv_full, preferred_element_type=F32) + bias
    ).astype(BF16)
    context, totals = attend(segments, qkv)
    attended = dot(context, out_full, 1, 1) + out_bias
    normal_one, inverse_one = norm_stats(x.astype(F32) + attended)
    hidden = normal_one * norm_gains[0] + norm_shifts[0]
    hidden_low = hidden.astype(BF16)
    if fits:
        activation, slope, branch = feed_forward(
            hidden_low, gathered, in_bias, in_part, out_part
        )
    else:
        in_full = gathered[:, :in_part].reshape(hidden_width, width)
        back_full = (
            gathered[:, in_part:]
            .reshape(devices, chunks, out_part, width)
            .transpose(0, 2, 1, 3)
            .reshape(width, hidden_width)
        )
        pre_act = dot(hidden_low, in_full, 1, 1) + in_bias
        cumulative, along = gelu_parts(pre_act)
        activation = (pre_act * cumulative).astype(BF16)
        slope = cumulative + along
        branch = dot(activation, back_full, 1, 1)
    branch = branch + back_bias
    normal_two, inverse_two = norm_stats(hidden + branch)
    out = (normal_two * norm_gains[1] + norm_shifts[1]).astype(BF16)

    error = out_cotangent.reshape(micro * local, width).astype(F32)
    grad_two = norm_back(normal_two, inverse_two, error, norm_gains[1])
    gain_two = jnp.sum(error * normal_two, axis=0)
    shift_two = jnp.sum(error, axis=0)
    grad_branch = grad_two.astype(BF16)
    if fits:
        grad_hidden, in_bias_sum, in_terms, back_terms = feed_backward(
            grad_branch, hidden_low, activation, slope, gathered, in_part, out_part
        )
        back_sum = lax.psum_scatter(back_terms, AXES, scatter_dimension=0, tiled=False)
        exchange = Halving(in_terms, dp_size)
        beside = exchange.step
    else:
        back_term = dot(grad_branch, activation, 0, 0).astype(BF16)
        grad_pre = (slope * dot(grad_branch, back_full, 1, 0)).astype(BF16)
        in_term = dot(grad_pre, hidden_low, 0, 0).astype(BF16)
        back_term = (
            back_term.reshape(devices, out_part, chunks, width)
            .transpose(0, 2, 1, 3)
            .reshape(devices, back_part, width)
        )
        terms = jnp.concatenate(
            [
                in_term.reshape(devices, in_part, width),
                back_term,
            ],
            axis=1,
        )
        grad_hidden = dot(grad_pre, in_full, 1, 0)
        in_bias_sum = jnp.sum(grad_pre.astype(F32), axis=0)
        summed = lax.psum_scatter(terms, AXES, scatter_dimension=0, tiled=False)
        in_sum, back_sum = summed[:in_part], summed[in_part:]

        def beside(values):
            return values

    grad_hidden = grad_two + grad_hidden
    grad_one = norm_back(normal_one, inverse_one, grad_hidden, norm_gains[0])
    gain_one = jnp.sum(grad_hidden * normal_one, axis=0)
    shift_one = jnp.sum(grad_hidden, axis=0)
    grad_attn = grad_one.astype(BF16)
    out_term = dot(grad_attn, context, 0, 0).astype(BF16)
    grad_context = beside(dot(grad_attn, out_full, 1, 0).astype(BF16))
    grad_qkv = beside(attend_back(segments, qkv, totals, grad_context))
    term = jnp.einsum("td,ctf->cdf", x, grad_qkv, preferred_element_type=F32)
    small = jnp.concatenate(
        [
            jnp.sum(grad_qkv[0].astype(F32), axis=0),
            jnp.sum(grad_qkv[2].astype(F32), axis=0),
            jnp.sum(grad_attn.astype(F32), axis=0),
            in_bias_sum.reshape(-1),
            jnp.sum(grad_branch.astype(F32), axis=0),
            gain_one,
            gain_two,
            shift_one,
            shift_two,
        ]
    )
    term, out_term, small = beside((term.astype(BF16), out_term, small))
    qkv_grad, out_grad, small, late = beside(
        (*reduce_projections(term, out_term, small.reshape(-1, 128), dp_size), grad_qkv)
    )
    small = small.reshape(-1)
    x_grad = grad_one + jnp.einsum(
        "ctf,cdf->td", late, qkv_full, preferred_element_type=F32
    )
    if fits:
        in_sum = exchange.total()
    in_sum, back_sum = in_sum.astype(F32), back_sum.astype(F32)
    cuts, at = [], 0
    for size in (2 * width, width, hidden_width, width, 2 * width, 2 * width):
        cuts.append(small[at : at + size])
        at += size
    return (
        out.reshape(tokens.shape),
        x_grad.reshape(tokens.shape),
        qkv_grad,
        cuts[0].reshape(2, width),
        out_grad.T,
        cuts[1],
        in_sum.T,
        cuts[2],
        back_sum.reshape(chunks, out_part, width)
        .transpose(0, 2, 1)
        .reshape(hidden_width, out_part),
        cuts[3],
        cuts[4].reshape(2, width),
        cuts[5].reshape(2, width),
    )


def solution(mesh):
    return jax.shard_map(
        functools.partial(
            on_device, dp_size=mesh.shape["dp"], head_size=mesh.shape["head"]
        ),
        mesh=mesh,
        in_specs=(
            P(None, AXES, None),
            P(None, "dp", None),
            P(None, "dp", "head"),
            P(),
            P(None, AXES),
            P(),
            P(None, AXES),
            P(),
            P(None, AXES),
            P(),
            P(),
            P(),
            P(None, AXES, None),
        ),
        out_specs=(
            P(None, AXES, None),
            P(None, AXES, None),
            P(None, "dp", "head"),
            P(),
            P(None, AXES),
            P(),
            P(None, AXES),
            P(),
            P(None, AXES),
            P(),
            P(),
            P(),
        ),
        check_vma=False,
    )
```

```python
import functools
import math

import jax
import jax.numpy as jnp
from jax import lax
from jax.experimental import pallas as pl
from jax.experimental.pallas import tpu as pltpu
from jax.sharding import PartitionSpec as P

HD = 64
NORM_EPS = 1e-05
MASKED = -1e30
AXES = ("dp", "head")
F32 = jnp.float32
BF16 = jnp.bfloat16
MESH = pl.DeviceIdType.MESH
TILE = 256


def dot(left, right, left_dim, right_dim):
    return lax.dot_general(
        left, right, (((left_dim,), (right_dim,)), ((), ())), preferred_element_type=F32
    )


def fill_mask(segment_row, segment_col, mask_ref):
    @pl.when(pl.program_id(1) == 0)
    def _():
        mask_ref[...] = jnp.where(segment_col[0] == segment_row[0], 0.0, MASKED)


def lane_halves(rows):
    lane = lax.broadcasted_iota(jnp.int32, (rows, 2 * HD), 1)
    return lane < HD


def attend_kernel(seg_row, seg_col, qkv_ref, context_ref, total_ref, mask_ref):
    fill_mask(seg_row, seg_col, mask_ref)
    queries = qkv_ref[0] * jnp.asarray(HD**-0.5, BF16)
    key_rows = qkv_ref[1]
    values = qkv_ref[2]
    first = lane_halves(key_rows.shape[0])
    parts = []
    for head in range(2):
        keys_own = jnp.where(first if head == 0 else ~first, key_rows, jnp.zeros_like(key_rows))
        scores = dot(keys_own, queries, 1, 1) + mask_ref[...]
        highest = jnp.max(scores, axis=0, keepdims=True)
        exponent = jnp.exp(scores - highest)
        totals = jnp.sum(exponent, axis=0, keepdims=True)
        low = (exponent * (1.0 / totals)).astype(BF16)
        total_ref[0, 0, head : head + 1, :] = highest + jnp.log(totals)
        parts.append(dot(values, low, 0, 0))
    joined = jnp.concatenate([parts[0][:HD], parts[1][HD:]], axis=0)
    context_ref[...] = joined.T.astype(BF16)


def attend_back_kernel(seg_row, seg_col, qkv_ref, total_ref, grad_ref, out_ref, mask_ref):
    fill_mask(seg_row, seg_col, mask_ref)
    scale = jnp.asarray(HD**-0.5, BF16)
    queries = qkv_ref[0] * scale
    key_rows = qkv_ref[1]
    key_scaled = key_rows * scale
    values = qkv_ref[2]
    grad = grad_ref[...]
    first = lane_halves(key_rows.shape[0])
    grad_queries, grad_keys, grad_values = [], [], []
    for head in range(2):
        own = first if head == 0 else ~first
        zero = jnp.zeros_like(key_rows)
        scores = dot(jnp.where(own, key_rows, zero), queries, 1, 1) + mask_ref[...]
        probs = jnp.exp(scores - total_ref[0, 0, head : head + 1, :])
        grad_probs = dot(jnp.where(own, values, zero), grad, 1, 1)
        weighted = jnp.sum(probs * grad_probs, axis=0, keepdims=True)
        grad_scores = (probs * (grad_probs - weighted)).astype(BF16)
        grad_values.append(dot(probs.astype(BF16), grad, 1, 0))
        grad_keys.append(dot(grad_scores, queries, 1, 0))
        grad_queries.append(dot(key_scaled, grad_scores, 0, 0))
    joined = jnp.concatenate([grad_queries[0][:HD], grad_queries[1][HD:]], axis=0)
    out_ref[0] = joined.T.astype(BF16)
    out_ref[1] = jnp.where(first, grad_keys[0], grad_keys[1]).astype(BF16)
    out_ref[2] = jnp.where(first, grad_values[0], grad_values[1]).astype(BF16)


def attention_specs(seq_len):
    return dict(
        row=pl.BlockSpec((1, 1, seq_len), lambda r, h: (r, 0, 0)),
        col=pl.BlockSpec((1, seq_len, 1), lambda r, h: (r, 0, 0)),
        three=pl.BlockSpec((3, seq_len, 2 * HD), lambda r, h: (0, r, h)),
        one=pl.BlockSpec((seq_len, 2 * HD), lambda r, h: (r, h)),
        total=pl.BlockSpec((1, 1, 8, seq_len), lambda r, h: (r, h, 0, 0)),
    )


def attend(segments, qkv):
    rows, seq_len = segments.shape
    pairs = qkv.shape[2] // (2 * HD)
    s = attention_specs(seq_len)
    area = rows * pairs * 2 * seq_len * seq_len
    return pl.pallas_call(
        attend_kernel,
        grid=(rows, pairs),
        in_specs=[s["row"], s["col"], s["three"]],
        out_specs=[s["one"], s["total"]],
        out_shape=[
            jax.ShapeDtypeStruct(qkv.shape[1:], BF16),
            jax.ShapeDtypeStruct((rows, pairs, 8, seq_len), F32),
        ],
        scratch_shapes=[pltpu.VMEM((seq_len, seq_len), F32)],
        cost_estimate=pl.CostEstimate(
            flops=area * 512, bytes_accessed=qkv.size * 3, transcendentals=area
        ),
        name="attend",
    )(segments[:, None, :], segments[:, :, None], qkv)


def attend_back(segments, qkv, totals, grad):
    rows, seq_len = segments.shape
    pairs = qkv.shape[2] // (2 * HD)
    s = attention_specs(seq_len)
    area = rows * pairs * 2 * seq_len * seq_len
    return pl.pallas_call(
        attend_back_kernel,
        grid=(rows, pairs),
        in_specs=[s["row"], s["col"], s["three"], s["total"], s["one"]],
        out_specs=s["three"],
        out_shape=jax.ShapeDtypeStruct(qkv.shape, BF16),
        scratch_shapes=[pltpu.VMEM((seq_len, seq_len), F32)],
        cost_estimate=pl.CostEstimate(
            flops=area * 1280, bytes_accessed=qkv.size * 5, transcendentals=area
        ),
        name="attend_back",
    )(segments[:, None, :], segments[:, :, None], qkv, totals, grad)


def gelu_parts(value, reciprocal=lambda v: 1.0 / v):
    size = jnp.abs(value)
    bell = jnp.exp2(value * value * (-0.5 / math.log(2.0)))
    t = reciprocal(1.0 + (0.3275911 / math.sqrt(2.0)) * size)
    series = 1.061405429 / 2
    for factor in (-1.453152027 / 2, 1.421413741 / 2, -0.284496736 / 2, 0.254829592 / 2):
        series = series * t + factor
    tail = series * t * bell
    cumulative = jnp.where(value < 0, tail, 1.0 - tail)
    return cumulative, value * bell * (1.0 / math.sqrt(2.0 * math.pi))


def forward_kernel(hidden_ref, in_ref, back_ref, bias_ref, act_ref, slope_ref, branch_ref):
    width = hidden_ref.shape[1]
    w_in = in_ref[...].reshape(-1, width)
    w_back = back_ref[...].reshape(width, -1)
    first = pl.program_id(0) == 0

    def body(tile, carry):
        rows = pl.ds(pl.multiple_of(tile * TILE, TILE), TILE)
        pre_act = dot(hidden_ref[rows, :], w_in, 1, 1) + bias_ref[...]
        cumulative, along = gelu_parts(pre_act, pl.reciprocal)
        activation = (pre_act * cumulative).astype(BF16)
        act_ref[rows, :] = activation
        slope_ref[rows, :] = cumulative + along
        branch = dot(activation, w_back, 1, 1)
        branch_ref[rows, :] = branch + jnp.where(first, 0.0, branch_ref[rows, :])
        return carry

    lax.fori_loop(0, hidden_ref.shape[0] // TILE, body, 0, unroll=2)


def weight_specs(gathered, in_part, out_part):
    devices, rows, width = gathered.shape
    chunks = in_part * devices // width
    return (
        pl.BlockSpec((devices // chunks, in_part, width), lambda c: (c, 0, 0)),
        pl.BlockSpec((devices, out_part, width), lambda c: (0, in_part // out_part + c, 0)),
    )


def feed_forward(hidden, gathered, bias, in_part, out_part):
    tokens, width = hidden.shape
    units = bias.shape[0]
    whole = pl.BlockSpec((tokens, width), lambda c: (0, 0))
    chunk = pl.BlockSpec((tokens, width), lambda c: (0, c))
    return pl.pallas_call(
        forward_kernel,
        grid=(units // width,),
        in_specs=[
            whole,
            *weight_specs(gathered, in_part, out_part),
            pl.BlockSpec((1, width), lambda c: (0, c)),
        ],
        out_specs=[chunk, chunk, whole],
        out_shape=[
            jax.ShapeDtypeStruct((tokens, units), BF16),
            jax.ShapeDtypeStruct((tokens, units), F32),
            jax.ShapeDtypeStruct((tokens, width), F32),
        ],
        cost_estimate=pl.CostEstimate(
            flops=4 * tokens * width * units,
            bytes_accessed=6 * tokens * units,
            transcendentals=2 * tokens * units,
        ),
        name="feed_forward",
    )(hidden, gathered, gathered, bias[None])


def backward_kernel(
    grad_ref,
    hidden_ref,
    act_ref,
    slope_ref,
    in_ref,
    back_ref,
    grad_hidden_ref,
    bias_ref,
    in_terms,
    back_terms,
    turned,
    grad_pre,
    in_tile,
    back_tile,
    sems,
):
    step, steps = pl.program_id(0), pl.num_programs(0)
    slot = step % 2
    tokens, width = hidden_ref.shape
    _, shards, in_part, _ = in_tile.shape
    devices, out_part = back_tile.shape[1:3]
    w_in = in_ref[...].reshape(-1, width)
    w_back = back_ref[...].reshape(width, -1)

    def copies(at, place):
        return (
            pltpu.make_async_copy(
                in_tile.at[place],
                in_terms.at[pl.ds(at * shards, shards)],
                sems.at[0, place],
            ),
            pltpu.make_async_copy(
                back_tile.at[place],
                back_terms.at[:, pl.ds(pl.multiple_of(at * out_part, 8), out_part)],
                sems.at[1, place],
            ),
        )

    @pl.when(step == 0)
    def _():
        turned[...] = grad_ref[...].T

    @pl.when(step >= 2)
    def _():
        for copy in copies(step - 2, slot):
            copy.wait()

    def body(tile, total):
        rows = pl.ds(pl.multiple_of(tile * TILE, TILE), TILE)
        grad = (slope_ref[rows, :] * dot(grad_ref[rows, :], w_back, 1, 0)).astype(BF16)
        grad_pre[rows, :] = grad
        term = dot(grad, w_in, 1, 0)
        grad_hidden_ref[rows, :] = term + jnp.where(step == 0, 0.0, grad_hidden_ref[rows, :])
        return total + jnp.sum(grad.astype(F32), axis=0, keepdims=True)

    bias_ref[...] = lax.fori_loop(0, tokens // TILE, body, jnp.zeros((1, width), F32))
    half = width // 2

    def weights(part, carry):
        span = pl.ds(pl.multiple_of(part * half, half), half)
        term = dot(grad_pre[:, span], hidden_ref[...], 0, 0)
        in_tile[slot, pl.ds(part * (shards // 2), shards // 2)] = term.reshape(
            shards // 2, in_part, width
        ).astype(BF16)
        term = dot(turned[span, :], act_ref[...], 1, 0)
        back_tile[slot, pl.ds(part * (devices // 2), devices // 2)] = term.reshape(
            devices // 2, out_part, width
        ).astype(BF16)
        return carry

    lax.fori_loop(0, 2, weights, 0)
    for copy in copies(step, slot):
        copy.start()

    @pl.when(step == steps - 1)
    def _():
        for copy in copies(step - 1, 1 - slot) + copies(step, slot):
            copy.wait()


class Halving:
    def __init__(self, terms, dp_size):
        count = dp_size.bit_length() - 1
        self.dp_size = dp_size
        self.orders = [list(reversed(order)) for order in exchange_orders(dp_size)]
        names = list(range(count - 1, -1, -1)) + ["head"]
        self.parts = [terms.reshape((2,) * (count + 1) + terms.shape[1:])]
        self.lefts = [names]
        self.at = 0

    def fold(self, held, left, bit):
        axis, size = ("head", 2) if bit == "head" else ("dp", self.dp_size)
        step = 1 if bit == "head" else 2**bit
        place, own = left.index(bit), own_bit(bit)
        give = lax.dynamic_index_in_dim(held, 1 - own, place, keepdims=False)
        keep = lax.dynamic_index_in_dim(held, own, place, keepdims=False)
        came = lax.ppermute(give, axis, [(i, i ^ step) for i in range(size)])
        return (keep, came), [b for b in left if b != bit]

    def step(self, values):
        if self.at == 1:
            half = self.parts[0].shape[-2] // 2
            self.parts = [self.parts[0][..., :half, :], self.parts[0][..., half:, :]]
            self.lefts = self.lefts * 2
        pairs = []
        for stream, part in enumerate(self.parts):
            pair, self.lefts[stream] = self.fold(
                part, self.lefts[stream], self.orders[stream][self.at]
            )
            pairs.append(pair)
        self.at += 1
        pairs, values = lax.optimization_barrier((pairs, values))
        self.parts = [
            (keep.astype(F32) + came.astype(F32)).astype(BF16) for keep, came in pairs
        ]
        return values

    def rest(self):
        return jnp.concatenate(self.parts, axis=-2)


def feed_backward(grad, hidden, activation, slope, gathered, in_part, out_part):
    tokens, width = hidden.shape
    units = activation.shape[1]
    devices = gathered.shape[0]
    shards = width // in_part
    whole = pl.BlockSpec((tokens, width), lambda c: (0, 0))
    chunk = pl.BlockSpec((tokens, width), lambda c: (0, c))
    return pl.pallas_call(
        backward_kernel,
        grid=(units // width,),
        in_specs=[whole, whole, chunk, chunk, *weight_specs(gathered, in_part, out_part)],
        out_specs=[
            whole,
            pl.BlockSpec((1, width), lambda c: (0, c)),
            pl.BlockSpec(memory_space=pl.ANY),
            pl.BlockSpec(memory_space=pl.ANY),
        ],
        out_shape=[
            jax.ShapeDtypeStruct((tokens, width), F32),
            jax.ShapeDtypeStruct((1, units), F32),
            jax.ShapeDtypeStruct((devices, in_part, width), BF16),
            jax.ShapeDtypeStruct((devices, units // width * out_part, width), BF16),
        ],
        scratch_shapes=[
            pltpu.VMEM((width, tokens), BF16),
            pltpu.VMEM((tokens, width), BF16),
            pltpu.VMEM((2, shards, in_part, width), BF16),
            pltpu.VMEM((2, devices, out_part, width), BF16),
            pltpu.SemaphoreType.DMA((2, 2)),
        ],
        cost_estimate=pl.CostEstimate(
            flops=8 * tokens * width * units, bytes_accessed=10 * tokens * units, transcendentals=0
        ),
        name="feed_backward",
    )(grad, hidden, activation, slope, gathered, gathered)


def norm_stats(residual):
    average = jnp.mean(residual, axis=-1, keepdims=True)
    centred = residual - average
    spread = jnp.mean(centred * centred, axis=-1, keepdims=True)
    inverse = lax.rsqrt(spread + NORM_EPS)
    return centred * inverse, inverse


def norm_back(normal, inverse, grad, gain):
    weighted = grad * gain
    along = jnp.mean(weighted * normal, axis=-1, keepdims=True)
    return inverse * (weighted - jnp.mean(weighted, axis=-1, keepdims=True) - normal * along)


def exchange_orders(dp_size):
    bits = list(range(dp_size.bit_length() - 2, -1, -1))
    return bits[:-1] + ["head", bits[-1]], bits[:-2] + ["head", bits[-2], bits[-1]]


def own_bit(bit):
    return lax.axis_index("head") if bit == "head" else (lax.axis_index("dp") // 2**bit) % 2


def partner_of(bit):
    index = lax.axis_index("head" if bit == "head" else "dp")
    step = 1 if bit == "head" else 2**bit
    return {"head" if bit == "head" else "dp": index + step - 2 * step * own_bit(bit)}


def meet(bits):
    barrier = pltpu.get_barrier_semaphore()
    for bit in bits:
        pl.semaphore_signal(barrier, 1, device_id=partner_of(bit), device_id_type=MESH)
    pl.semaphore_wait(barrier, len(bits))


def lanes_of(half, width):
    return pl.ds(pl.multiple_of(half * width, width), width)


def gather_kernel(dp_size, qkv_ref, out_ref, qkv_full, out_full, own_sem, send_sem, recv_sem):
    orders = exchange_orders(dp_size)
    bits = [bit for bit in orders[0] if bit != "head"]
    width = qkv_ref.shape[2]
    meet(orders[0])

    def qkv_view(kinds, done):
        index = tuple(slice(None) if bit in done else own_bit(bit) for bit in bits)
        lanes = slice(None) if "head" in done else lanes_of(own_bit("head"), width)
        return qkv_full.at[(kinds,) + index + (slice(None), lanes)]

    def out_view(done):
        return out_full.at[
            tuple(slice(None) if bit in done else own_bit(bit) for bit in bits + ["head"])
        ]

    own = [
        pltpu.make_async_copy(qkv_ref, qkv_view(slice(None), ()), own_sem.at[0]),
        pltpu.make_async_copy(out_ref, out_view(()), own_sem.at[1]),
    ]
    for copy in own:
        copy.start()
    for copy in own:
        copy.wait()
    for step in range(len(orders[0])):
        copies = []
        for stream in range(3):
            order = orders[0] if stream == 0 else orders[1]
            done = order[:step]
            if stream == 2:
                view = out_view(done)
            else:
                view = qkv_view(slice(0, 2) if stream == 0 else slice(2, 3), done)
            copies.append(
                pltpu.make_async_remote_copy(
                    src_ref=view,
                    dst_ref=view,
                    send_sem=send_sem.at[step, stream],
                    recv_sem=recv_sem.at[step, stream],
                    device_id=partner_of(order[step]),
                    device_id_type=MESH,
                )
            )
        for copy in copies:
            copy.start()
        for copy in copies:
            copy.wait()


def gather_projections(qkv_shard, out_shard, dp_size):
    _, part, own_width = qkv_shard.shape
    bits = (2,) * (dp_size.bit_length() - 1)
    steps = len(bits) + 1
    vmem = pl.BlockSpec(memory_space=pltpu.VMEM)
    qkv_full, out_full = pl.pallas_call(
        functools.partial(gather_kernel, dp_size),
        out_shape=[
            jax.ShapeDtypeStruct((3,) + bits + (part, 2 * own_width), BF16),
            jax.ShapeDtypeStruct(bits + (2,) + out_shard.shape, BF16),
        ],
        in_specs=[vmem, vmem],
        out_specs=[vmem, vmem],
        scratch_shapes=[
            pltpu.SemaphoreType.DMA((2,)),
            pltpu.SemaphoreType.DMA((steps, 3)),
            pltpu.SemaphoreType.DMA((steps, 3)),
        ],
        compiler_params=pltpu.CompilerParams(collective_id=1, has_side_effects=True),
        cost_estimate=pl.CostEstimate(flops=0, bytes_accessed=2**27, transcendentals=0),
        name="gather_projections",
    )(qkv_shard, out_shard)
    return (
        qkv_full.reshape(3, dp_size * part, 2 * own_width),
        out_full.reshape(dp_size * 2 * out_shard.shape[0], out_shard.shape[1]),
    )


def reduce_kernel(
    dp_size,
    qkv_ref,
    out_ref,
    small_ref,
    tail_ref,
    grad_qkv_hbm,
    weights_hbm,
    grad_one_hbm,
    qkv_sum,
    out_sum,
    small_sum,
    tail_sum,
    x_grad,
    small_held,
    small_in,
    tail_held,
    tail_first,
    tail_last,
    grad_qkv,
    weights,
    load_sem,
    *scratch,
):
    steps = len(exchange_orders(dp_size)[0])
    arrived, held = scratch[: 3 * steps], scratch[3 * steps : -2]
    send_sem, recv_sem = scratch[-2:]
    loads = [
        pltpu.make_async_copy(grad_qkv_hbm, grad_qkv, load_sem.at[0]),
        pltpu.make_async_copy(weights_hbm, weights, load_sem.at[1]),
        pltpu.make_async_copy(grad_one_hbm, x_grad, load_sem.at[2]),
    ]
    for load in loads:
        load.start()
    small_held[0] = small_ref[...]

    def add_products(tile, carry):
        rows = pl.ds(pl.multiple_of(tile * TILE, TILE), TILE)
        total = x_grad[rows, :]
        for kind in range(3):
            total += dot(grad_qkv[kind, rows, :], weights[kind], 1, 1)
        x_grad[rows, :] = total
        return carry

    orders = [list(reversed(order)) for order in exchange_orders(dp_size)]
    meet(orders[0])
    bits = [bit for bit in orders[0] if bit != "head"]
    bits.sort(reverse=True)
    width = qkv_sum.shape[2]

    def view(ref, kinds, done, bit, half):
        index = tuple(half if b == bit else slice(None) for b in bits if b not in done)
        if kinds is None:
            if "head" not in done:
                index += (half if bit == "head" else slice(None),)
            return index
        lanes = lanes_of(half, width) if bit == "head" else slice(None)
        return (kinds,) + index + (slice(None), lanes)

    for step in range(steps):
        copies, mine = [], []
        for stream in range(3):
            order = orders[0] if stream == 0 else orders[1]
            bit, done = order[step], order[:step]
            if step == 0:
                source = out_ref if stream == 2 else qkv_ref
                kinds = (slice(0, 2), slice(2, 3), None)[stream]
            else:
                source = held[3 * (step - 1) + stream]
                kinds = None if stream == 2 else slice(None)
            target = arrived[3 * step + stream]
            copies.append(
                pltpu.make_async_remote_copy(
                    src_ref=source.at[view(source, kinds, done, bit, 1 - own_bit(bit))],
                    dst_ref=target,
                    send_sem=send_sem.at[step, stream],
                    recv_sem=recv_sem.at[step, stream],
                    device_id=partner_of(bit),
                    device_id_type=MESH,
                )
            )
            mine.append((source, view(source, kinds, done, bit, own_bit(bit)), target))
        copies.append(
            pltpu.make_async_remote_copy(
                src_ref=small_held.at[step],
                dst_ref=small_in.at[step],
                send_sem=send_sem.at[step, 3],
                recv_sem=recv_sem.at[step, 3],
                device_id=partner_of(orders[0][step]),
                device_id_type=MESH,
            )
        )
        if step >= steps - 2:
            bit = orders[0][step]
            first = step == steps - 2
            copies.append(
                pltpu.make_async_remote_copy(
                    src_ref=tail_ref.at[:, 1 - own_bit(bit)]
                    if first
                    else tail_held.at[1 - own_bit(bit)],
                    dst_ref=tail_first if first else tail_last,
                    send_sem=send_sem.at[step, 4],
                    recv_sem=recv_sem.at[step, 4],
                    device_id=partner_of(bit),
                    device_id_type=MESH,
                )
            )
        for copy in copies:
            copy.start()
        if step == 1:
            for load in loads:
                load.wait()
            lax.fori_loop(0, x_grad.shape[0] // TILE, add_products, 0)
        for stream in range(3):
            copies[stream].wait()
            source, index, target = mine[stream]
            total = source[index].astype(F32) + target[...].astype(F32)
            if step < steps - 1:
                held[3 * step + stream][...] = total.astype(BF16)
            elif stream == 2:
                out_sum[...] = total
            elif stream == 0:
                qkv_sum[0:2] = total
            else:
                qkv_sum[2:3] = total
        copies[3].wait()
        small_held[step + 1] = small_held[step] + small_in[step]
        if step == steps - 2:
            copies[4].wait()
            tail_held[...] = (
                tail_ref[:, own_bit(bit)].astype(F32) + tail_first[...].astype(F32)
            ).astype(BF16)
        elif step == steps - 1:
            copies[4].wait()
            tail_sum[...] = tail_held[own_bit(bit)].astype(F32) + tail_last[...].astype(F32)
    small_sum[...] = small_held[steps]


def reduce_projections(qkv_term, out_term, small, tail, grad_qkv, weights, grad_one, dp_size):
    count = dp_size.bit_length() - 1
    part, own_width = qkv_term.shape[1] // dp_size, qkv_term.shape[2] // 2
    out_part = out_term.shape[0] // (2 * dp_size)
    orders = [list(reversed(order)) for order in exchange_orders(dp_size)]
    shapes = []
    for step in range(count + 1):
        for stream in range(3):
            done = orders[0 if stream == 0 else 1][: step + 1]
            left = (2,) * (count - sum(bit != "head" for bit in done))
            if stream == 2:
                head = () if "head" in done else (2,)
                shapes.append(left + head + (out_part, out_term.shape[1]))
            else:
                wide = own_width if "head" in done else 2 * own_width
                shapes.append(((2, 1)[stream],) + left + (part, wide))
    vmem = pl.BlockSpec(memory_space=pltpu.VMEM)
    buffers = [pltpu.VMEM(shape, BF16) for shape in shapes]
    return pl.pallas_call(
        functools.partial(reduce_kernel, dp_size),
        out_shape=[
            jax.ShapeDtypeStruct((3, part, own_width), F32),
            jax.ShapeDtypeStruct((out_part, out_term.shape[1]), F32),
            jax.ShapeDtypeStruct(small.shape, F32),
            jax.ShapeDtypeStruct(tail.shape[2:], F32),
            jax.ShapeDtypeStruct(grad_one.shape, F32),
        ],
        in_specs=[vmem] * 4 + [pl.BlockSpec(memory_space=pl.ANY)] * 3,
        out_specs=[vmem] * 5,
        scratch_shapes=[
            pltpu.VMEM((count + 2,) + small.shape, F32),
            pltpu.VMEM((count + 1,) + small.shape, F32),
            pltpu.VMEM(tail.shape[1:], BF16),
            pltpu.VMEM(tail.shape[1:], BF16),
            pltpu.VMEM(tail.shape[2:], BF16),
            pltpu.VMEM(grad_qkv.shape, BF16),
            pltpu.VMEM(weights.shape, BF16),
            pltpu.SemaphoreType.DMA((3,)),
        ]
        + buffers
        + buffers[: 3 * count]
        + [pltpu.SemaphoreType.DMA((count + 1, 5)), pltpu.SemaphoreType.DMA((count + 1, 5))],
        compiler_params=pltpu.CompilerParams(collective_id=2, has_side_effects=True),
        cost_estimate=pl.CostEstimate(flops=0, bytes_accessed=2**27, transcendentals=0),
        name="reduce_projections",
    )(
        qkv_term.reshape((3,) + (2,) * count + (part, 2 * own_width)),
        out_term.reshape((2,) * (count + 1) + (out_part, out_term.shape[1])),
        small,
        tail,
        grad_qkv,
        weights,
        grad_one,
    )


def sum_everywhere(x, sizes):
    steps = sum(size.bit_length() - 1 for _, size in sizes)
    return pl.pallas_call(
        functools.partial(sum_kernel, sizes),
        out_shape=jax.ShapeDtypeStruct(x.shape, x.dtype),
        in_specs=[pl.BlockSpec(memory_space=pltpu.VMEM)],
        out_specs=pl.BlockSpec(memory_space=pltpu.VMEM),
        scratch_shapes=[
            pltpu.VMEM((steps + 1,) + x.shape, x.dtype),
            pltpu.VMEM((steps,) + x.shape, x.dtype),
            pltpu.SemaphoreType.DMA((steps,)),
            pltpu.SemaphoreType.DMA((steps,)),
        ],
        compiler_params=pltpu.CompilerParams(collective_id=0, has_side_effects=True),
        name="sum_everywhere",
    )(x)


def on_device(
    tokens,
    segment_ids,
    w_qkv,
    qv_bias,
    w_out,
    out_bias,
    w_in,
    in_bias,
    w_back,
    back_bias,
    norm_gains,
    norm_shifts,
    out_cotangent,
    *,
    dp_size,
    head_size,
):
    micro, local, width = tokens.shape
    seq_len = segment_ids.shape[2]
    own_rows = local // seq_len

    devices = dp_size * head_size
    hidden_width = in_bias.shape[0]
    out_part, in_part = width // devices, hidden_width // devices
    chunks = hidden_width // width
    back_part = chunks * out_part
    packed = jnp.concatenate(
        [
            w_in.T,
            w_back.reshape(chunks, width, out_part).transpose(0, 2, 1).reshape(back_part, width),
        ]
    )
    gathered = lax.all_gather(packed, AXES, axis=0, tiled=False)
    fits = in_part % 16 == 0 and out_part % 8 == 0 and dp_size >= 8
    qkv_full, out_full = gather_projections(w_qkv, w_out.T, dp_size)

    x = tokens.reshape(micro * local, width)
    segments = lax.dynamic_slice_in_dim(
        segment_ids, lax.axis_index("head") * own_rows, own_rows, 1
    ).reshape(micro * own_rows, seq_len)
    bias = jnp.stack([qv_bias[0], jnp.zeros_like(qv_bias[0]), qv_bias[1]])[:, None, :]
    qkv = (
        jnp.einsum("td,cdf->ctf", x, qkv_full, preferred_element_type=F32) + bias
    ).astype(BF16)
    context, totals = attend(segments, qkv)
    attended = dot(context, out_full, 1, 1) + out_bias
    normal_one, inverse_one = norm_stats(x.astype(F32) + attended)
    hidden = normal_one * norm_gains[0] + norm_shifts[0]
    hidden_low = hidden.astype(BF16)
    if fits:
        activation, slope, branch = feed_forward(
            hidden_low, gathered, in_bias, in_part, out_part
        )
    else:
        in_full = gathered[:, :in_part].reshape(hidden_width, width)
        back_full = (
            gathered[:, in_part:]
            .reshape(devices, chunks, out_part, width)
            .transpose(0, 2, 1, 3)
            .reshape(width, hidden_width)
        )
        pre_act = dot(hidden_low, in_full, 1, 1) + in_bias
        cumulative, along = gelu_parts(pre_act)
        activation = (pre_act * cumulative).astype(BF16)
        slope = cumulative + along
        branch = dot(activation, back_full, 1, 1)
    branch = branch + back_bias
    normal_two, inverse_two = norm_stats(hidden + branch)
    out = (normal_two * norm_gains[1] + norm_shifts[1]).astype(BF16)

    error = out_cotangent.reshape(micro * local, width).astype(F32)
    grad_two = norm_back(normal_two, inverse_two, error, norm_gains[1])
    gain_two = jnp.sum(error * normal_two, axis=0)
    shift_two = jnp.sum(error, axis=0)
    grad_branch = grad_two.astype(BF16)
    if fits:
        grad_hidden, in_bias_sum, in_terms, back_terms = feed_backward(
            grad_branch, hidden_low, activation, slope, gathered, in_part, out_part
        )
        back_sum = lax.psum_scatter(back_terms, AXES, scatter_dimension=0, tiled=False)
        exchange = Halving(in_terms, dp_size)
        beside = exchange.step
    else:
        back_term = dot(grad_branch, activation, 0, 0).astype(BF16)
        grad_pre = (slope * dot(grad_branch, back_full, 1, 0)).astype(BF16)
        in_term = dot(grad_pre, hidden_low, 0, 0).astype(BF16)
        back_term = (
            back_term.reshape(devices, out_part, chunks, width)
            .transpose(0, 2, 1, 3)
            .reshape(devices, back_part, width)
        )
        terms = jnp.concatenate(
            [
                in_term.reshape(devices, in_part, width),
                back_term,
            ],
            axis=1,
        )
        grad_hidden = dot(grad_pre, in_full, 1, 0)
        in_bias_sum = jnp.sum(grad_pre.astype(F32), axis=0)
        summed = lax.psum_scatter(terms, AXES, scatter_dimension=0, tiled=False)
        in_sum, back_sum = summed[:in_part], summed[in_part:]

        def beside(values):
            return values

    grad_hidden = grad_two + grad_hidden
    grad_one = norm_back(normal_one, inverse_one, grad_hidden, norm_gains[0])
    gain_one = jnp.sum(grad_hidden * normal_one, axis=0)
    shift_one = jnp.sum(grad_hidden, axis=0)
    grad_attn = grad_one.astype(BF16)
    out_term = dot(grad_attn, context, 0, 0).astype(BF16)
    grad_context = beside(dot(grad_attn, out_full, 1, 0).astype(BF16))
    grad_qkv = beside(attend_back(segments, qkv, totals, grad_context))
    term = jnp.einsum("td,ctf->cdf", x, grad_qkv, preferred_element_type=F32)
    small = jnp.concatenate(
        [
            jnp.sum(grad_qkv[0].astype(F32), axis=0),
            jnp.sum(grad_qkv[2].astype(F32), axis=0),
            jnp.sum(grad_attn.astype(F32), axis=0),
            in_bias_sum.reshape(-1),
            jnp.sum(grad_branch.astype(F32), axis=0),
            gain_one,
            gain_two,
            shift_one,
            shift_two,
        ]
    )
    term, out_term, small = beside((term.astype(BF16), out_term, small))
    rest = exchange.rest() if fits else jnp.zeros((2, 2, 16, width), BF16)
    qkv_grad, out_grad, small, in_rest, x_grad = reduce_projections(
        term, out_term, small.reshape(-1, 128), rest, grad_qkv, qkv_full, grad_one, dp_size
    )
    in_sum = (in_rest if fits else in_sum).astype(F32)
    back_sum = back_sum.astype(F32)
    small = small.reshape(-1)
    cuts, at = [], 0
    for size in (2 * width, width, hidden_width, width, 2 * width, 2 * width):
        cuts.append(small[at : at + size])
        at += size
    return (
        out.reshape(tokens.shape),
        x_grad.reshape(tokens.shape),
        qkv_grad,
        cuts[0].reshape(2, width),
        out_grad.T,
        cuts[1],
        in_sum.T,
        cuts[2],
        back_sum.reshape(chunks, out_part, width)
        .transpose(0, 2, 1)
        .reshape(hidden_width, out_part),
        cuts[3],
        cuts[4].reshape(2, width),
        cuts[5].reshape(2, width),
    )


def solution(mesh):
    return jax.shard_map(
        functools.partial(
            on_device, dp_size=mesh.shape["dp"], head_size=mesh.shape["head"]
        ),
        mesh=mesh,
        in_specs=(
            P(None, AXES, None),
            P(None, "dp", None),
            P(None, "dp", "head"),
            P(),
            P(None, AXES),
            P(),
            P(None, AXES),
            P(),
            P(None, AXES),
            P(),
            P(),
            P(),
            P(None, AXES, None),
        ),
        out_specs=(
            P(None, AXES, None),
            P(None, AXES, None),
            P(None, "dp", "head"),
            P(),
            P(None, AXES),
            P(),
            P(None, AXES),
            P(),
            P(None, AXES),
            P(),
            P(),
            P(),
        ),
        check_vma=False,
    )
```

```python
import functools
import math

import jax
import jax.numpy as jnp
from jax import lax
from jax.experimental import pallas as pl
from jax.experimental.pallas import tpu as pltpu
from jax.sharding import PartitionSpec as P

HD = 64
NORM_EPS = 1e-05
MASKED = -1e30
AXES = ("dp", "head")
F32 = jnp.float32
BF16 = jnp.bfloat16
MESH = pl.DeviceIdType.MESH
TILE = 256


def dot(left, right, left_dim, right_dim):
    return lax.dot_general(
        left, right, (((left_dim,), (right_dim,)), ((), ())), preferred_element_type=F32
    )


def fill_mask(segment_row, segment_col, mask_ref):
    @pl.when(pl.program_id(1) == 0)
    def _():
        mask_ref[...] = jnp.where(segment_col[0] == segment_row[0], 0.0, MASKED)


def lane_halves(rows):
    lane = lax.broadcasted_iota(jnp.int32, (rows, 2 * HD), 1)
    return lane < HD


def attend_kernel(seg_row, seg_col, qkv_ref, context_ref, total_ref, mask_ref):
    fill_mask(seg_row, seg_col, mask_ref)
    queries = qkv_ref[0] * jnp.asarray(HD**-0.5, BF16)
    key_rows = qkv_ref[1]
    values = qkv_ref[2]
    first = lane_halves(key_rows.shape[0])
    parts = []
    for head in range(2):
        keys_own = jnp.where(first if head == 0 else ~first, key_rows, jnp.zeros_like(key_rows))
        scores = dot(keys_own, queries, 1, 1) + mask_ref[...]
        highest = jnp.max(scores, axis=0, keepdims=True)
        exponent = jnp.exp(scores - highest)
        totals = jnp.sum(exponent, axis=0, keepdims=True)
        low = (exponent * (1.0 / totals)).astype(BF16)
        total_ref[0, 0, head : head + 1, :] = highest + jnp.log(totals)
        parts.append(dot(values, low, 0, 0))
    joined = jnp.concatenate([parts[0][:HD], parts[1][HD:]], axis=0)
    context_ref[...] = joined.T.astype(BF16)


def attend_back_kernel(seg_row, seg_col, qkv_ref, total_ref, grad_ref, out_ref, mask_ref):
    fill_mask(seg_row, seg_col, mask_ref)
    scale = jnp.asarray(HD**-0.5, BF16)
    queries = qkv_ref[0] * scale
    key_rows = qkv_ref[1]
    key_scaled = key_rows * scale
    values = qkv_ref[2]
    grad = grad_ref[...]
    first = lane_halves(key_rows.shape[0])
    grad_queries, grad_keys, grad_values = [], [], []
    for head in range(2):
        own = first if head == 0 else ~first
        zero = jnp.zeros_like(key_rows)
        scores = dot(jnp.where(own, key_rows, zero), queries, 1, 1) + mask_ref[...]
        probs = jnp.exp(scores - total_ref[0, 0, head : head + 1, :])
        grad_probs = dot(jnp.where(own, values, zero), grad, 1, 1)
        weighted = jnp.sum(probs * grad_probs, axis=0, keepdims=True)
        grad_scores = (probs * (grad_probs - weighted)).astype(BF16)
        grad_values.append(dot(probs.astype(BF16), grad, 1, 0))
        grad_keys.append(dot(grad_scores, queries, 1, 0))
        grad_queries.append(dot(key_scaled, grad_scores, 0, 0))
    joined = jnp.concatenate([grad_queries[0][:HD], grad_queries[1][HD:]], axis=0)
    out_ref[0] = joined.T.astype(BF16)
    out_ref[1] = jnp.where(first, grad_keys[0], grad_keys[1]).astype(BF16)
    out_ref[2] = jnp.where(first, grad_values[0], grad_values[1]).astype(BF16)


def attention_specs(seq_len):
    return dict(
        row=pl.BlockSpec((1, 1, seq_len), lambda r, h: (r, 0, 0)),
        col=pl.BlockSpec((1, seq_len, 1), lambda r, h: (r, 0, 0)),
        three=pl.BlockSpec((3, seq_len, 2 * HD), lambda r, h: (0, r, h)),
        one=pl.BlockSpec((seq_len, 2 * HD), lambda r, h: (r, h)),
        total=pl.BlockSpec((1, 1, 8, seq_len), lambda r, h: (r, h, 0, 0)),
    )


def attend(segments, qkv):
    rows, seq_len = segments.shape
    pairs = qkv.shape[2] // (2 * HD)
    s = attention_specs(seq_len)
    area = rows * pairs * 2 * seq_len * seq_len
    return pl.pallas_call(
        attend_kernel,
        grid=(rows, pairs),
        in_specs=[s["row"], s["col"], s["three"]],
        out_specs=[s["one"], s["total"]],
        out_shape=[
            jax.ShapeDtypeStruct(qkv.shape[1:], BF16),
            jax.ShapeDtypeStruct((rows, pairs, 8, seq_len), F32),
        ],
        scratch_shapes=[pltpu.VMEM((seq_len, seq_len), F32)],
        cost_estimate=pl.CostEstimate(
            flops=area * 512, bytes_accessed=qkv.size * 3, transcendentals=area
        ),
        name="attend",
    )(segments[:, None, :], segments[:, :, None], qkv)


def attend_back(segments, qkv, totals, grad):
    rows, seq_len = segments.shape
    pairs = qkv.shape[2] // (2 * HD)
    s = attention_specs(seq_len)
    area = rows * pairs * 2 * seq_len * seq_len
    return pl.pallas_call(
        attend_back_kernel,
        grid=(rows, pairs),
        in_specs=[s["row"], s["col"], s["three"], s["total"], s["one"]],
        out_specs=s["three"],
        out_shape=jax.ShapeDtypeStruct(qkv.shape, BF16),
        scratch_shapes=[pltpu.VMEM((seq_len, seq_len), F32)],
        cost_estimate=pl.CostEstimate(
            flops=area * 1280, bytes_accessed=qkv.size * 5, transcendentals=area
        ),
        name="attend_back",
    )(segments[:, None, :], segments[:, :, None], qkv, totals, grad)


def gelu_parts(value, reciprocal=lambda v: 1.0 / v):
    size = jnp.abs(value)
    bell = jnp.exp2(value * value * (-0.5 / math.log(2.0)))
    t = reciprocal(1.0 + (0.3275911 / math.sqrt(2.0)) * size)
    series = 1.061405429 / 2
    for factor in (-1.453152027 / 2, 1.421413741 / 2, -0.284496736 / 2, 0.254829592 / 2):
        series = series * t + factor
    tail = series * t * bell
    cumulative = jnp.where(value < 0, tail, 1.0 - tail)
    return cumulative, value * bell * (1.0 / math.sqrt(2.0 * math.pi))


def forward_kernel(hidden_ref, in_ref, back_ref, bias_ref, act_ref, slope_ref, branch_ref):
    width = hidden_ref.shape[1]
    w_in = in_ref[...].reshape(-1, width)
    w_back = back_ref[...].reshape(width, -1)
    first = pl.program_id(0) == 0

    def body(tile, carry):
        rows = pl.ds(pl.multiple_of(tile * TILE, TILE), TILE)
        pre_act = dot(hidden_ref[rows, :], w_in, 1, 1) + bias_ref[...]
        cumulative, along = gelu_parts(pre_act, pl.reciprocal)
        activation = (pre_act * cumulative).astype(BF16)
        act_ref[rows, :] = activation
        slope_ref[rows, :] = cumulative + along
        branch = dot(activation, w_back, 1, 1)
        branch_ref[rows, :] = branch + jnp.where(first, 0.0, branch_ref[rows, :])
        return carry

    lax.fori_loop(0, hidden_ref.shape[0] // TILE, body, 0, unroll=2)


def weight_specs(gathered, in_part, out_part):
    devices, rows, width = gathered.shape
    chunks = in_part * devices // width
    return (
        pl.BlockSpec((devices // chunks, in_part, width), lambda c: (c, 0, 0)),
        pl.BlockSpec((devices, out_part, width), lambda c: (0, in_part // out_part + c, 0)),
    )


def feed_forward(hidden, gathered, bias, in_part, out_part):
    tokens, width = hidden.shape
    units = bias.shape[0]
    whole = pl.BlockSpec((tokens, width), lambda c: (0, 0))
    chunk = pl.BlockSpec((tokens, width), lambda c: (0, c))
    return pl.pallas_call(
        forward_kernel,
        grid=(units // width,),
        in_specs=[
            whole,
            *weight_specs(gathered, in_part, out_part),
            pl.BlockSpec((1, width), lambda c: (0, c)),
        ],
        out_specs=[chunk, chunk, whole],
        out_shape=[
            jax.ShapeDtypeStruct((tokens, units), BF16),
            jax.ShapeDtypeStruct((tokens, units), F32),
            jax.ShapeDtypeStruct((tokens, width), F32),
        ],
        cost_estimate=pl.CostEstimate(
            flops=4 * tokens * width * units,
            bytes_accessed=6 * tokens * units,
            transcendentals=2 * tokens * units,
        ),
        name="feed_forward",
    )(hidden, gathered, gathered, bias[None])


def backward_kernel(
    grad_ref,
    hidden_ref,
    act_ref,
    slope_ref,
    in_ref,
    back_ref,
    grad_hidden_ref,
    bias_ref,
    in_terms,
    back_terms,
    turned,
    grad_pre,
    in_tile,
    back_tile,
    sems,
):
    step, steps = pl.program_id(0), pl.num_programs(0)
    slot = step % 2
    tokens, width = hidden_ref.shape
    _, shards, in_part, _ = in_tile.shape
    devices, out_part = back_tile.shape[1:3]
    w_in = in_ref[...].reshape(-1, width)
    w_back = back_ref[...].reshape(width, -1)

    def copies(at, place):
        return (
            pltpu.make_async_copy(
                in_tile.at[place],
                in_terms.at[pl.ds(at * shards, shards)],
                sems.at[0, place],
            ),
            pltpu.make_async_copy(
                back_tile.at[place],
                back_terms.at[:, pl.ds(pl.multiple_of(at * out_part, 8), out_part)],
                sems.at[1, place],
            ),
        )

    @pl.when(step == 0)
    def _():
        turned[...] = grad_ref[...].T

    @pl.when(step >= 2)
    def _():
        for copy in copies(step - 2, slot):
            copy.wait()

    def body(tile, total):
        rows = pl.ds(pl.multiple_of(tile * TILE, TILE), TILE)
        grad = (slope_ref[rows, :] * dot(grad_ref[rows, :], w_back, 1, 0)).astype(BF16)
        grad_pre[rows, :] = grad
        term = dot(grad, w_in, 1, 0)
        grad_hidden_ref[rows, :] = term + jnp.where(step == 0, 0.0, grad_hidden_ref[rows, :])
        return total + jnp.sum(grad.astype(F32), axis=0, keepdims=True)

    bias_ref[...] = lax.fori_loop(0, tokens // TILE, body, jnp.zeros((1, width), F32))
    half = width // 2

    def weights(part, carry):
        span = pl.ds(pl.multiple_of(part * half, half), half)
        term = dot(grad_pre[:, span], hidden_ref[...], 0, 0)
        in_tile[slot, pl.ds(part * (shards // 2), shards // 2)] = term.reshape(
            shards // 2, in_part, width
        ).astype(BF16)
        term = dot(turned[span, :], act_ref[...], 1, 0)
        back_tile[slot, pl.ds(part * (devices // 2), devices // 2)] = term.reshape(
            devices // 2, out_part, width
        ).astype(BF16)
        return carry

    lax.fori_loop(0, 2, weights, 0)
    for copy in copies(step, slot):
        copy.start()

    @pl.when(step == steps - 1)
    def _():
        for copy in copies(step - 1, 1 - slot) + copies(step, slot):
            copy.wait()


class Halving:
    def __init__(self, terms, dp_size):
        count = dp_size.bit_length() - 1
        self.dp_size = dp_size
        self.orders = [list(reversed(order)) for order in exchange_orders(dp_size)]
        names = list(range(count - 1, -1, -1)) + ["head"]
        self.parts = [terms.reshape((2,) * (count + 1) + terms.shape[1:])]
        self.lefts = [names]
        self.at = 0

    def fold(self, held, left, bit):
        axis, size = ("head", 2) if bit == "head" else ("dp", self.dp_size)
        step = 1 if bit == "head" else 2**bit
        place, own = left.index(bit), own_bit(bit)
        give = lax.dynamic_index_in_dim(held, 1 - own, place, keepdims=False)
        keep = lax.dynamic_index_in_dim(held, own, place, keepdims=False)
        came = lax.ppermute(give, axis, [(i, i ^ step) for i in range(size)])
        return (keep, came), [b for b in left if b != bit]

    def step(self, values):
        if self.at == 1:
            half = self.parts[0].shape[-2] // 2
            self.parts = [self.parts[0][..., :half, :], self.parts[0][..., half:, :]]
            self.lefts = self.lefts * 2
        pairs = []
        for stream, part in enumerate(self.parts):
            pair, self.lefts[stream] = self.fold(
                part, self.lefts[stream], self.orders[stream][self.at]
            )
            pairs.append(pair)
        self.at += 1
        pairs, values = lax.optimization_barrier((pairs, values))
        self.parts = [
            (keep.astype(F32) + came.astype(F32)).astype(BF16) for keep, came in pairs
        ]
        return values

    def rest(self):
        return jnp.concatenate(self.parts, axis=-2)


def feed_backward(grad, hidden, activation, slope, gathered, in_part, out_part):
    tokens, width = hidden.shape
    units = activation.shape[1]
    devices = gathered.shape[0]
    shards = width // in_part
    whole = pl.BlockSpec((tokens, width), lambda c: (0, 0))
    chunk = pl.BlockSpec((tokens, width), lambda c: (0, c))
    return pl.pallas_call(
        backward_kernel,
        grid=(units // width,),
        in_specs=[whole, whole, chunk, chunk, *weight_specs(gathered, in_part, out_part)],
        out_specs=[
            whole,
            pl.BlockSpec((1, width), lambda c: (0, c)),
            pl.BlockSpec(memory_space=pl.ANY),
            pl.BlockSpec(memory_space=pl.ANY),
        ],
        out_shape=[
            jax.ShapeDtypeStruct((tokens, width), F32),
            jax.ShapeDtypeStruct((1, units), F32),
            jax.ShapeDtypeStruct((devices, in_part, width), BF16),
            jax.ShapeDtypeStruct((devices, units // width * out_part, width), BF16),
        ],
        scratch_shapes=[
            pltpu.VMEM((width, tokens), BF16),
            pltpu.VMEM((tokens, width), BF16),
            pltpu.VMEM((2, shards, in_part, width), BF16),
            pltpu.VMEM((2, devices, out_part, width), BF16),
            pltpu.SemaphoreType.DMA((2, 2)),
        ],
        cost_estimate=pl.CostEstimate(
            flops=8 * tokens * width * units, bytes_accessed=10 * tokens * units, transcendentals=0
        ),
        name="feed_backward",
    )(grad, hidden, activation, slope, gathered, gathered)


def norm_stats(residual):
    average = jnp.mean(residual, axis=-1, keepdims=True)
    centred = residual - average
    spread = jnp.mean(centred * centred, axis=-1, keepdims=True)
    inverse = lax.rsqrt(spread + NORM_EPS)
    return centred * inverse, inverse


def norm_back(normal, inverse, grad, gain):
    weighted = grad * gain
    along = jnp.mean(weighted * normal, axis=-1, keepdims=True)
    return inverse * (weighted - jnp.mean(weighted, axis=-1, keepdims=True) - normal * along)


def exchange_orders(dp_size):
    bits = list(range(dp_size.bit_length() - 2, -1, -1))
    return bits[:-1] + ["head", bits[-1]], bits[:-2] + ["head", bits[-2], bits[-1]]


def own_bit(bit):
    return lax.axis_index("head") if bit == "head" else (lax.axis_index("dp") // 2**bit) % 2


def partner_of(bit):
    index = lax.axis_index("head" if bit == "head" else "dp")
    step = 1 if bit == "head" else 2**bit
    return {"head" if bit == "head" else "dp": index + step - 2 * step * own_bit(bit)}


def meet(bits):
    barrier = pltpu.get_barrier_semaphore()
    for bit in bits:
        pl.semaphore_signal(barrier, 1, device_id=partner_of(bit), device_id_type=MESH)
    pl.semaphore_wait(barrier, len(bits))


def lanes_of(half, width):
    return pl.ds(pl.multiple_of(half * width, width), width)


def gather_kernel(dp_size, qkv_ref, out_ref, qkv_full, out_full, own_sem, send_sem, recv_sem):
    orders = exchange_orders(dp_size)
    bits = [bit for bit in orders[0] if bit != "head"]
    width = qkv_ref.shape[2]
    meet(orders[0])

    def qkv_view(kinds, done):
        index = tuple(slice(None) if bit in done else own_bit(bit) for bit in bits)
        lanes = slice(None) if "head" in done else lanes_of(own_bit("head"), width)
        return qkv_full.at[(kinds,) + index + (slice(None), lanes)]

    def out_view(done):
        return out_full.at[
            tuple(slice(None) if bit in done else own_bit(bit) for bit in bits + ["head"])
        ]

    own = [
        pltpu.make_async_copy(qkv_ref, qkv_view(slice(None), ()), own_sem.at[0]),
        pltpu.make_async_copy(out_ref, out_view(()), own_sem.at[1]),
    ]
    for copy in own:
        copy.start()
    for copy in own:
        copy.wait()
    for step in range(len(orders[0])):
        copies = []
        for stream in range(3):
            order = orders[0] if stream == 0 else orders[1]
            done = order[:step]
            if stream == 2:
                view = out_view(done)
            else:
                view = qkv_view(slice(0, 2) if stream == 0 else slice(2, 3), done)
            copies.append(
                pltpu.make_async_remote_copy(
                    src_ref=view,
                    dst_ref=view,
                    send_sem=send_sem.at[step, stream],
                    recv_sem=recv_sem.at[step, stream],
                    device_id=partner_of(order[step]),
                    device_id_type=MESH,
                )
            )
        for copy in copies:
            copy.start()
        for copy in copies:
            copy.wait()


def gather_projections(qkv_shard, out_shard, dp_size):
    _, part, own_width = qkv_shard.shape
    bits = (2,) * (dp_size.bit_length() - 1)
    steps = len(bits) + 1
    vmem = pl.BlockSpec(memory_space=pltpu.VMEM)
    qkv_full, out_full = pl.pallas_call(
        functools.partial(gather_kernel, dp_size),
        out_shape=[
            jax.ShapeDtypeStruct((3,) + bits + (part, 2 * own_width), BF16),
            jax.ShapeDtypeStruct(bits + (2,) + out_shard.shape, BF16),
        ],
        in_specs=[vmem, vmem],
        out_specs=[vmem, vmem],
        scratch_shapes=[
            pltpu.SemaphoreType.DMA((2,)),
            pltpu.SemaphoreType.DMA((steps, 3)),
            pltpu.SemaphoreType.DMA((steps, 3)),
        ],
        compiler_params=pltpu.CompilerParams(collective_id=1, has_side_effects=True),
        cost_estimate=pl.CostEstimate(flops=0, bytes_accessed=2**27, transcendentals=0),
        name="gather_projections",
    )(qkv_shard, out_shard)
    return (
        qkv_full.reshape(3, dp_size * part, 2 * own_width),
        out_full.reshape(dp_size * 2 * out_shard.shape[0], out_shard.shape[1]),
    )


def reduce_kernel(
    dp_size,
    qkv_ref,
    out_ref,
    small_ref,
    tail_ref,
    grad_qkv_hbm,
    weights_hbm,
    grad_one_hbm,
    qkv_sum,
    out_sum,
    small_sum,
    tail_sum,
    x_grad,
    small_held,
    small_in,
    tail_held,
    tail_first,
    tail_last,
    grad_qkv,
    weights,
    load_sem,
    *scratch,
):
    steps = len(exchange_orders(dp_size)[0])
    arrived, held = scratch[: 3 * steps], scratch[3 * steps : -2]
    send_sem, recv_sem = scratch[-2:]
    loads = [
        pltpu.make_async_copy(grad_qkv_hbm, grad_qkv, load_sem.at[0]),
        pltpu.make_async_copy(weights_hbm, weights, load_sem.at[1]),
        pltpu.make_async_copy(grad_one_hbm, x_grad, load_sem.at[2]),
    ]
    for load in loads:
        load.start()
    small_held[0] = small_ref[...]

    def add_products(tile, carry):
        rows = pl.ds(pl.multiple_of(tile * TILE, TILE), TILE)
        total = x_grad[rows, :]
        for kind in range(3):
            total += dot(grad_qkv[kind, rows, :], weights[kind], 1, 1)
        x_grad[rows, :] = total
        return carry

    orders = [list(reversed(order)) for order in exchange_orders(dp_size)]
    meet(orders[0])
    bits = [bit for bit in orders[0] if bit != "head"]
    bits.sort(reverse=True)
    width = qkv_sum.shape[2]

    def view(ref, kinds, done, bit, half):
        index = tuple(half if b == bit else slice(None) for b in bits if b not in done)
        if kinds is None:
            if "head" not in done:
                index += (half if bit == "head" else slice(None),)
            return index
        lanes = lanes_of(half, width) if bit == "head" else slice(None)
        return (kinds,) + index + (slice(None), lanes)

    for step in range(steps):
        copies, mine = [], []
        for stream in range(3):
            order = orders[0] if stream == 0 else orders[1]
            bit, done = order[step], order[:step]
            if step == 0:
                source = out_ref if stream == 2 else qkv_ref
                kinds = (slice(0, 2), slice(2, 3), None)[stream]
            else:
                source = held[3 * (step - 1) + stream]
                kinds = None if stream == 2 else slice(None)
            target = arrived[3 * step + stream]
            copies.append(
                pltpu.make_async_remote_copy(
                    src_ref=source.at[view(source, kinds, done, bit, 1 - own_bit(bit))],
                    dst_ref=target,
                    send_sem=send_sem.at[step, stream],
                    recv_sem=recv_sem.at[step, stream],
                    device_id=partner_of(bit),
                    device_id_type=MESH,
                )
            )
            mine.append((source, view(source, kinds, done, bit, own_bit(bit)), target))
        copies.append(
            pltpu.make_async_remote_copy(
                src_ref=small_held.at[step],
                dst_ref=small_in.at[step],
                send_sem=send_sem.at[step, 3],
                recv_sem=recv_sem.at[step, 3],
                device_id=partner_of(orders[0][step]),
                device_id_type=MESH,
            )
        )
        if step in (1, 2):
            tail_bit = orders[0][steps - 3 + step]
            first = step == 1
            copies.append(
                pltpu.make_async_remote_copy(
                    src_ref=tail_ref.at[:, 1 - own_bit(tail_bit)]
                    if first
                    else tail_held.at[1 - own_bit(tail_bit)],
                    dst_ref=tail_first if first else tail_last,
                    send_sem=send_sem.at[step, 4],
                    recv_sem=recv_sem.at[step, 4],
                    device_id=partner_of(tail_bit),
                    device_id_type=MESH,
                )
            )
        for copy in copies:
            copy.start()
        if step == 1:
            for load in loads:
                load.wait()
            lax.fori_loop(0, x_grad.shape[0] // TILE, add_products, 0)
        for stream in range(3):
            copies[stream].wait()
            source, index, target = mine[stream]
            total = source[index].astype(F32) + target[...].astype(F32)
            if step < steps - 1:
                held[3 * step + stream][...] = total.astype(BF16)
            elif stream == 2:
                out_sum[...] = total
            elif stream == 0:
                qkv_sum[0:2] = total
            else:
                qkv_sum[2:3] = total
        copies[3].wait()
        small_held[step + 1] = small_held[step] + small_in[step]
        if step == 1:
            copies[4].wait()
            tail_held[...] = (
                tail_ref[:, own_bit(tail_bit)].astype(F32) + tail_first[...].astype(F32)
            ).astype(BF16)
        elif step == 2:
            copies[4].wait()
            tail_sum[...] = tail_held[own_bit(tail_bit)].astype(F32) + tail_last[...].astype(F32)
    small_sum[...] = small_held[steps]


def reduce_projections(qkv_term, out_term, small, tail, grad_qkv, weights, grad_one, dp_size):
    count = dp_size.bit_length() - 1
    part, own_width = qkv_term.shape[1] // dp_size, qkv_term.shape[2] // 2
    out_part = out_term.shape[0] // (2 * dp_size)
    orders = [list(reversed(order)) for order in exchange_orders(dp_size)]
    shapes = []
    for step in range(count + 1):
        for stream in range(3):
            done = orders[0 if stream == 0 else 1][: step + 1]
            left = (2,) * (count - sum(bit != "head" for bit in done))
            if stream == 2:
                head = () if "head" in done else (2,)
                shapes.append(left + head + (out_part, out_term.shape[1]))
            else:
                wide = own_width if "head" in done else 2 * own_width
                shapes.append(((2, 1)[stream],) + left + (part, wide))
    vmem = pl.BlockSpec(memory_space=pltpu.VMEM)
    buffers = [pltpu.VMEM(shape, BF16) for shape in shapes]
    return pl.pallas_call(
        functools.partial(reduce_kernel, dp_size),
        out_shape=[
            jax.ShapeDtypeStruct((3, part, own_width), F32),
            jax.ShapeDtypeStruct((out_part, out_term.shape[1]), F32),
            jax.ShapeDtypeStruct(small.shape, F32),
            jax.ShapeDtypeStruct(tail.shape[2:], F32),
            jax.ShapeDtypeStruct(grad_one.shape, F32),
        ],
        in_specs=[vmem] * 4 + [pl.BlockSpec(memory_space=pl.ANY)] * 3,
        out_specs=[vmem] * 5,
        scratch_shapes=[
            pltpu.VMEM((count + 2,) + small.shape, F32),
            pltpu.VMEM((count + 1,) + small.shape, F32),
            pltpu.VMEM(tail.shape[1:], BF16),
            pltpu.VMEM(tail.shape[1:], BF16),
            pltpu.VMEM(tail.shape[2:], BF16),
            pltpu.VMEM(grad_qkv.shape, BF16),
            pltpu.VMEM(weights.shape, BF16),
            pltpu.SemaphoreType.DMA((3,)),
        ]
        + buffers
        + buffers[: 3 * count]
        + [pltpu.SemaphoreType.DMA((count + 1, 5)), pltpu.SemaphoreType.DMA((count + 1, 5))],
        compiler_params=pltpu.CompilerParams(collective_id=2, has_side_effects=True),
        cost_estimate=pl.CostEstimate(flops=0, bytes_accessed=2**27, transcendentals=0),
        name="reduce_projections",
    )(
        qkv_term.reshape((3,) + (2,) * count + (part, 2 * own_width)),
        out_term.reshape((2,) * (count + 1) + (out_part, out_term.shape[1])),
        small,
        tail,
        grad_qkv,
        weights,
        grad_one,
    )


def sum_everywhere(x, sizes):
    steps = sum(size.bit_length() - 1 for _, size in sizes)
    return pl.pallas_call(
        functools.partial(sum_kernel, sizes),
        out_shape=jax.ShapeDtypeStruct(x.shape, x.dtype),
        in_specs=[pl.BlockSpec(memory_space=pltpu.VMEM)],
        out_specs=pl.BlockSpec(memory_space=pltpu.VMEM),
        scratch_shapes=[
            pltpu.VMEM((steps + 1,) + x.shape, x.dtype),
            pltpu.VMEM((steps,) + x.shape, x.dtype),
            pltpu.SemaphoreType.DMA((steps,)),
            pltpu.SemaphoreType.DMA((steps,)),
        ],
        compiler_params=pltpu.CompilerParams(collective_id=0, has_side_effects=True),
        name="sum_everywhere",
    )(x)


def on_device(
    tokens,
    segment_ids,
    w_qkv,
    qv_bias,
    w_out,
    out_bias,
    w_in,
    in_bias,
    w_back,
    back_bias,
    norm_gains,
    norm_shifts,
    out_cotangent,
    *,
    dp_size,
    head_size,
):
    micro, local, width = tokens.shape
    seq_len = segment_ids.shape[2]
    own_rows = local // seq_len

    devices = dp_size * head_size
    hidden_width = in_bias.shape[0]
    out_part, in_part = width // devices, hidden_width // devices
    chunks = hidden_width // width
    back_part = chunks * out_part
    packed = jnp.concatenate(
        [
            w_in.T,
            w_back.reshape(chunks, width, out_part).transpose(0, 2, 1).reshape(back_part, width),
        ]
    )
    gathered = lax.all_gather(packed, AXES, axis=0, tiled=False)
    fits = in_part % 16 == 0 and out_part % 8 == 0 and dp_size >= 8
    qkv_full, out_full = gather_projections(w_qkv, w_out.T, dp_size)

    x = tokens.reshape(micro * local, width)
    segments = lax.dynamic_slice_in_dim(
        segment_ids, lax.axis_index("head") * own_rows, own_rows, 1
    ).reshape(micro * own_rows, seq_len)
    bias = jnp.stack([qv_bias[0], jnp.zeros_like(qv_bias[0]), qv_bias[1]])[:, None, :]
    qkv = (
        jnp.einsum("td,cdf->ctf", x, qkv_full, preferred_element_type=F32) + bias
    ).astype(BF16)
    context, totals = attend(segments, qkv)
    attended = dot(context, out_full, 1, 1) + out_bias
    normal_one, inverse_one = norm_stats(x.astype(F32) + attended)
    hidden = normal_one * norm_gains[0] + norm_shifts[0]
    hidden_low = hidden.astype(BF16)
    if fits:
        activation, slope, branch = feed_forward(
            hidden_low, gathered, in_bias, in_part, out_part
        )
    else:
        in_full = gathered[:, :in_part].reshape(hidden_width, width)
        back_full = (
            gathered[:, in_part:]
            .reshape(devices, chunks, out_part, width)
            .transpose(0, 2, 1, 3)
            .reshape(width, hidden_width)
        )
        pre_act = dot(hidden_low, in_full, 1, 1) + in_bias
        cumulative, along = gelu_parts(pre_act)
        activation = (pre_act * cumulative).astype(BF16)
        slope = cumulative + along
        branch = dot(activation, back_full, 1, 1)
    branch = branch + back_bias
    normal_two, inverse_two = norm_stats(hidden + branch)
    out = (normal_two * norm_gains[1] + norm_shifts[1]).astype(BF16)

    error = out_cotangent.reshape(micro * local, width).astype(F32)
    grad_two = norm_back(normal_two, inverse_two, error, norm_gains[1])
    gain_two = jnp.sum(error * normal_two, axis=0)
    shift_two = jnp.sum(error, axis=0)
    grad_branch = grad_two.astype(BF16)
    if fits:
        grad_hidden, in_bias_sum, in_terms, back_terms = feed_backward(
            grad_branch, hidden_low, activation, slope, gathered, in_part, out_part
        )
        back_sum = lax.psum_scatter(back_terms, AXES, scatter_dimension=0, tiled=False)
        exchange = Halving(in_terms, dp_size)
        beside = exchange.step
    else:
        back_term = dot(grad_branch, activation, 0, 0).astype(BF16)
        grad_pre = (slope * dot(grad_branch, back_full, 1, 0)).astype(BF16)
        in_term = dot(grad_pre, hidden_low, 0, 0).astype(BF16)
        back_term = (
            back_term.reshape(devices, out_part, chunks, width)
            .transpose(0, 2, 1, 3)
            .reshape(devices, back_part, width)
        )
        terms = jnp.concatenate(
            [
                in_term.reshape(devices, in_part, width),
                back_term,
            ],
            axis=1,
        )
        grad_hidden = dot(grad_pre, in_full, 1, 0)
        in_bias_sum = jnp.sum(grad_pre.astype(F32), axis=0)
        summed = lax.psum_scatter(terms, AXES, scatter_dimension=0, tiled=False)
        in_sum, back_sum = summed[:in_part], summed[in_part:]

        def beside(values):
            return values

    grad_hidden = grad_two + grad_hidden
    grad_one = norm_back(normal_one, inverse_one, grad_hidden, norm_gains[0])
    gain_one = jnp.sum(grad_hidden * normal_one, axis=0)
    shift_one = jnp.sum(grad_hidden, axis=0)
    grad_attn = grad_one.astype(BF16)
    out_term = dot(grad_attn, context, 0, 0).astype(BF16)
    grad_context = beside(dot(grad_attn, out_full, 1, 0).astype(BF16))
    grad_qkv = beside(attend_back(segments, qkv, totals, grad_context))
    term = jnp.einsum("td,ctf->cdf", x, grad_qkv, preferred_element_type=F32)
    small = jnp.concatenate(
        [
            jnp.sum(grad_qkv[0].astype(F32), axis=0),
            jnp.sum(grad_qkv[2].astype(F32), axis=0),
            jnp.sum(grad_attn.astype(F32), axis=0),
            in_bias_sum.reshape(-1),
            jnp.sum(grad_branch.astype(F32), axis=0),
            gain_one,
            gain_two,
            shift_one,
            shift_two,
        ]
    )
    term, out_term, small = beside((term.astype(BF16), out_term, small))
    rest = exchange.rest() if fits else jnp.zeros((2, 2, 16, width), BF16)
    qkv_grad, out_grad, small, in_rest, x_grad = reduce_projections(
        term, out_term, small.reshape(-1, 128), rest, grad_qkv, qkv_full, grad_one, dp_size
    )
    in_sum = (in_rest if fits else in_sum).astype(F32)
    back_sum = back_sum.astype(F32)
    small = small.reshape(-1)
    cuts, at = [], 0
    for size in (2 * width, width, hidden_width, width, 2 * width, 2 * width):
        cuts.append(small[at : at + size])
        at += size
    return (
        out.reshape(tokens.shape),
        x_grad.reshape(tokens.shape),
        qkv_grad,
        cuts[0].reshape(2, width),
        out_grad.T,
        cuts[1],
        in_sum.T,
        cuts[2],
        back_sum.reshape(chunks, out_part, width)
        .transpose(0, 2, 1)
        .reshape(hidden_width, out_part),
        cuts[3],
        cuts[4].reshape(2, width),
        cuts[5].reshape(2, width),
    )


def solution(mesh):
    return jax.shard_map(
        functools.partial(
            on_device, dp_size=mesh.shape["dp"], head_size=mesh.shape["head"]
        ),
        mesh=mesh,
        in_specs=(
            P(None, AXES, None),
            P(None, "dp", None),
            P(None, "dp", "head"),
            P(),
            P(None, AXES),
            P(),
            P(None, AXES),
            P(),
            P(None, AXES),
            P(),
            P(),
            P(),
            P(None, AXES, None),
        ),
        out_specs=(
            P(None, AXES, None),
            P(None, AXES, None),
            P(None, "dp", "head"),
            P(),
            P(None, AXES),
            P(),
            P(None, AXES),
            P(),
            P(None, AXES),
            P(),
            P(),
            P(),
        ),
        check_vma=False,
    )
```
